512 devices in a mesh: lon: 64 (over z, y_lo, core), lat: 8 (over x, y_hi).
Axes of the slice: x: 4, y: 8 (y_hi: 2, y_lo: 4; y = y_hi * 4 + y_lo), z: 8, core: 2. Of those that a mesh axis runs over, the one named last changes fastest.
Arguments:
- pressure: float32 [128, 1024, 1024], P(None, 'lon', 'lat'), may hold values from -10 to 10
- ocean_mask: int32 [1024, 1024], P('lon', 'lat'), may hold values 0 or 1
Outputs:
- modes: float32 [128, 3, 1024, 1024], P(None, None, 'lon', 'lat')
- factor_r: float32 [128, 128], replicated
The draws below stay inside these ranges and needn't reach their ends.
All inputs are finite; a program needn't handle non-finite values. No bound on the sum of `ocean_mask` on one device may be relied on, other than what follows from the above.
Results may differ from the reference program's by a relative error of at most 0.0003.
Values sent between devices are 32-bit elements; how exact they have to be, the bound alone decides.
A program may use at most 64 MiB of HBM per device.

```python
import math
import jax
import jax.numpy as jnp
from jax import lax

SNAPS = 128
PASSES = 4
NLON = 1024
NLAT = 1024
ROWS = 3145728


def draw_pressure(key, part):
    subkeys = jax.random.split(jax.random.fold_in(key, 7919), 4)
    pattern_count = 6
    longitude = jnp.arange(NLON, dtype=jnp.float32)[:, None]
    latitude = jnp.arange(NLAT, dtype=jnp.float32)[None, :]
    chosen = jax.random.permutation(subkeys[0], 12)[:pattern_count]
    wave_lon = (chosen % 4 + 1).astype(jnp.float32)
    wave_lat = (chosen // 4 + 1).astype(jnp.float32)
    phases = jax.random.uniform(subkeys[1], (pattern_count, 2), jnp.float32, -math.pi, math.pi)
    decay_rate = 0.6 ** jnp.arange(pattern_count, dtype=jnp.float32)
    amplitude = jax.random.truncated_normal(subkeys[2], -4.0, 4.0, (SNAPS, pattern_count), jnp.float32)
    noise_field = 0.05 * jax.random.truncated_normal(subkeys[3], -4.0, 4.0, (SNAPS, NLON, NLAT), jnp.float32)
    summed = noise_field
    for which in range(pattern_count):
        along_lon = jnp.cos(2.0 * math.pi * wave_lon[which] * longitude / NLON + phases[which, 0])
        along_lat = jnp.cos(math.pi * wave_lat[which] * (latitude + 0.5) / NLAT + phases[which, 1])
        pattern = along_lon * along_lat
        weight_row = decay_rate[which] * amplitude[:, which]
        summed = summed + weight_row[:, None, None] * pattern[None, :, :]
    return summed.astype(jnp.float32)


def with_ends(result, key, low, top_value):
    longest = result.shape.index(max(result.shape))
    spots = []
    for shift in (0, 1):
        where = [jax.random.randint(jax.random.fold_in(key, axis), (), 0, length) for axis, length in enumerate(result.shape)]
        where[longest] = (where[longest] + shift) % result.shape[longest]
        spots.append(tuple(where))
    return result.at[spots[0]].set(low).at[spots[1]].set(top_value)


def setup_inputs(seed: int = 0) -> dict:
    seeds = jax.random.split(jax.random.key(seed), 3)
    return {
        "pressure": draw_pressure(jax.random.fold_in(seeds[2], 71), 0),
        "ocean_mask": with_ends((jax.random.randint(seeds[1], (NLON, NLAT), 0, 10) < 7).astype(jnp.int32), jax.random.fold_in(seeds[1], 1), 0, 1),
    }


def sweep_lon(field, mask):
    left = jnp.roll(field, 1, axis=1)
    right = jnp.roll(field, -1, axis=1)
    mask_left = jnp.roll(mask, 1, axis=0)
    mask_right = jnp.roll(mask, -1, axis=0)
    return mask * (field + 0.25 * (mask_left * (left - field) + mask_right * (right - field)))

def sweep_lat(field, mask):
    padded = jnp.pad(field, ((0, 0), (0, 0), (1, 1)))
    mask_pad = jnp.pad(mask, ((0, 0), (1, 1)))
    left = padded[:, :, :-2]
    right = padded[:, :, 2:]
    return mask * (field + 0.25 * (mask_pad[:, :-2] * (left - field) + mask_pad[:, 2:] * (right - field)))

def orthonormalize(flat):
    gram = lax.dot_general(flat.astype(jnp.float32), flat.astype(jnp.float32), (((1,), (1,)), ((), ())), precision=lax.Precision.HIGHEST, preferred_element_type=jnp.float32)
    lower = jnp.linalg.cholesky(gram)
    eye = jnp.eye(gram.shape[0], dtype=jnp.float32)
    inverse = jax.scipy.linalg.solve_triangular(lower, eye, lower=True)
    return (jnp.dot(inverse.astype(jnp.float32), flat.astype(jnp.float32), precision=lax.Precision.HIGHEST, preferred_element_type=jnp.float32), lower)

def reference(pressure, ocean_mask):
    mask = ocean_mask.astype(jnp.float32)
    field = mask * pressure
    for step in range(PASSES):
        field = sweep_lon(field, mask)
        field = sweep_lat(field, mask)
    grad_lon = 0.5 * mask * (jnp.roll(field, -1, axis=1) - jnp.roll(field, 1, axis=1))
    padded = jnp.pad(field, ((0, 0), (0, 0), (1, 1)))
    grad_lat = 0.5 * mask * (padded[:, :, 2:] - padded[:, :, :-2])
    stacked = jnp.stack([field, grad_lon, grad_lat], axis=1)
    flat = stacked.reshape(SNAPS, -1)
    first, lower_one = orthonormalize(flat)
    second, lower_two = orthonormalize(first)
    scale = jnp.sqrt(jnp.float32(ROWS))
    modes = (second * scale).reshape(SNAPS, 3, NLON, NLAT)
    factor_r = jnp.dot(lower_two.T.astype(jnp.float32), lower_one.T.astype(jnp.float32), precision=lax.Precision.HIGHEST, preferred_element_type=jnp.float32) / scale
    return (modes, factor_r)
```

```python
import functools

import jax
import jax.numpy as jnp
from jax import lax
from jax.experimental import pallas as pl
from jax.experimental.pallas import tpu as pltpu
from jax.sharding import PartitionSpec as P

PASSES = 4
MARGIN = PASSES + 1
CORES = 2
Y_LOW = 4
Y_HIGH = 2
MESH = pl.DeviceIdType.MESH
HIGHEST = lax.Precision.HIGHEST


class Place:
    def __init__(self, n_lon, n_lat):
        self.n_lon, self.n_lat = n_lon, n_lat
        self.n_z = n_lon // (Y_LOW * CORES)
        self.n_x = n_lat // Y_HIGH
        self.size_a = self.n_z * CORES
        self.size_b = n_lat * Y_LOW
        self.lon = lax.axis_index("lon")
        self.lat = lax.axis_index("lat")
        core = lax.rem(self.lon, CORES)
        pair = lax.div(self.lon, CORES)
        y_low = lax.rem(pair, Y_LOW)
        z = lax.div(pair, Y_LOW)
        self.core, self.y_low, self.z = core, y_low, z
        self.rank_a = z * CORES + core
        self.rank_b = self.lat * Y_LOW + y_low

    def peer_a(self, step):
        rank = lax.rem(self.rank_a + step, self.size_a)
        lon = (lax.div(rank, CORES) * Y_LOW + self.y_low) * CORES + lax.rem(rank, CORES)
        return rank, (lon, self.lat)

    def peer_b(self, step):
        rank = lax.rem(self.rank_b + step, self.size_b)
        lon = (self.z * Y_LOW + lax.rem(rank, Y_LOW)) * CORES + self.core
        return rank, (lon, lax.div(rank, Y_LOW))

    def near(self, dlon, dlat):
        return (
            lax.rem(self.lon + dlon + self.n_lon, self.n_lon),
            lax.rem(self.lat + dlat + self.n_lat, self.n_lat),
        )


def greet(place, others):
    barrier = pltpu.get_barrier_semaphore()
    for device in others:
        pl.semaphore_signal(barrier, inc=1, device_id=device, device_id_type=MESH)

    def greet_a(step, _):
        pl.semaphore_signal(barrier, inc=1, device_id=place.peer_a(step)[1], device_id_type=MESH)
        return 0

    def greet_b(step, _):
        pl.semaphore_signal(barrier, inc=1, device_id=place.peer_b(step)[1], device_id_type=MESH)
        return 0

    lax.fori_loop(1, place.size_a, greet_a, 0)
    lax.fori_loop(1, place.size_b, greet_b, 0)
    return len(others) + place.size_a + place.size_b - 2


def all_reduce(place, part, slots_a, slots_b, total, sems):
    send_a, recv_a, send_b, recv_b, send_c, recv_c = sems
    mine = place.rank_a

    def copy_a(step, recv_rank):
        rank, device = place.peer_a(step)
        return pltpu.make_async_remote_copy(
            src_ref=part.at[rank],
            dst_ref=slots_a.at[mine],
            send_sem=send_a.at[rank],
            recv_sem=recv_a.at[recv_rank],
            device_id=device,
            device_id_type=MESH,
        )

    def copy_b(step, recv_rank):
        rank, device = place.peer_b(step)
        return pltpu.make_async_remote_copy(
            src_ref=slots_b.at[place.rank_b],
            dst_ref=slots_b.at[place.rank_b],
            send_sem=send_b.at[rank],
            recv_sem=recv_b.at[recv_rank],
            device_id=device,
            device_id_type=MESH,
        )

    def copy_c(step, recv_rank):
        rank, device = place.peer_a(step)
        return pltpu.make_async_remote_copy(
            src_ref=total.at[mine],
            dst_ref=total.at[mine],
            send_sem=send_c.at[rank],
            recv_sem=recv_c.at[recv_rank],
            device_id=device,
            device_id_type=MESH,
        )

    def start(copy, rank, size):
        def body(step, _):
            copy(step, rank).start()
            return 0

        lax.fori_loop(1, size, body, 0)

    def finish(copy, peer, size):
        def body(step, _):
            rank, _ = peer(step)
            copy(step, rank).wait_recv()
            return 0

        lax.fori_loop(1, size, body, 0)

    def drain(copy, rank, size):
        def body(step, _):
            copy(step, rank).wait_send()
            return 0

        lax.fori_loop(1, size, body, 0)

    start(copy_a, mine, place.size_a)
    slots_a[mine] = part[mine]
    finish(copy_a, place.peer_a, place.size_a)
    slots_b[place.rank_b] = jnp.sum(slots_a[...], axis=0)
    start(copy_b, place.rank_b, place.size_b)
    finish(copy_b, place.peer_b, place.size_b)
    total[mine] = jnp.sum(slots_b[...], axis=0)
    start(copy_c, mine, place.size_a)
    finish(copy_c, place.peer_a, place.size_a)
    drain(copy_a, mine, place.size_a)
    drain(copy_b, place.rank_b, place.size_b)
    drain(copy_c, mine, place.size_a)


def reduce_scratch(size_a, size_b, snaps):
    rows = snaps // size_a
    return [
        pltpu.VMEM((size_a, rows, snaps), jnp.float32),
        pltpu.VMEM((size_a, rows, snaps), jnp.float32),
        pltpu.VMEM((size_b, rows, snaps), jnp.float32),
        pltpu.SemaphoreType.DMA((size_a,)),
        pltpu.SemaphoreType.DMA((size_a,)),
        pltpu.SemaphoreType.DMA((size_b,)),
        pltpu.SemaphoreType.DMA((size_b,)),
        pltpu.SemaphoreType.DMA((size_a,)),
        pltpu.SemaphoreType.DMA((size_a,)),
    ]


NEIGHBOURS = [(a, b) for a in (-1, 0, 1) for b in (-1, 0, 1) if (a, b) != (0, 0)]


def first_kernel(
    n_lon, n_lat,
    p_ref, mask_ref, flat_ref, gram_ref,
    raw, wide_mask, even, odd, quarter, keep_lon, keep_lat, halves, flat,
    part, slots_a, slots_b, sa, ra, sb, rb, sc, rc,
    send_near, recv_near, send_mask, recv_mask, out_sem,
):
    place = Place(n_lon, n_lat)
    clon, clat = mask_ref.shape
    snaps = raw.shape[2]
    base = 8
    wide = clat + 2 * base
    rows = clon + 2 * MARGIN
    expected = greet(place, [place.near(a, b) for a, b in NEIGHBOURS])

    lon0, lat0 = 8, clat
    wide_mask[lon0 : lon0 + clon, lat0 : lat0 + clat] = mask_ref[...].astype(jnp.float32)

    def turn(row):
        raw[MARGIN + row, base : base + clat, :] = p_ref[pl.ds(row, snaps, stride=clon), :].T

    edge = sorted(set(range(MARGIN)) | set(range(clon - MARGIN, clon)))
    for row in edge:
        turn(row)
    for row in range(clon):
        if row not in edge:
            turn(row)

    pl.semaphore_wait(pltpu.get_barrier_semaphore(), expected)

    def span(delta, own_at, own, margin):
        if delta == 0:
            return pl.ds(own_at, own), pl.ds(own_at, own)
        if delta > 0:
            return pl.ds(own_at + own - margin, margin), pl.ds(own_at - margin, margin)
        return pl.ds(own_at, margin), pl.ds(own_at + own, margin)

    copies = []
    for index, (a, b) in enumerate(NEIGHBOURS):
        src_lon, dst_lon = span(a, MARGIN, clon, MARGIN)
        src_lat, dst_lat = span(b, base, clat, base)
        copies.append(
            pltpu.make_async_remote_copy(
                src_ref=raw.at[src_lon, src_lat, :],
                dst_ref=raw.at[dst_lon, dst_lat, :],
                send_sem=send_near.at[index],
                recv_sem=recv_near.at[index],
                device_id=place.near(a, b),
                device_id_type=MESH,
            )
        )
        src_lon, dst_lon = span(a, lon0, clon, 8)
        src_lat, dst_lat = span(b, lat0, clat, clat)
        copies.append(
            pltpu.make_async_remote_copy(
                src_ref=wide_mask.at[src_lon, src_lat],
                dst_ref=wide_mask.at[dst_lon, dst_lat],
                send_sem=send_mask.at[index],
                recv_sem=recv_mask.at[index],
                device_id=place.near(a, b),
                device_id_type=MESH,
            )
        )
    for copy in copies:
        copy.start()
    for copy in copies:
        copy.wait_recv()

    low = jnp.where(place.lat > 0, 1.0, 0.0)
    high = jnp.where(place.lat < n_lat - 1, 1.0, 0.0)
    turned = jnp.concatenate(
        [
            wide_mask[:, 0:clat].T[clat - base :, :] * low,
            wide_mask[:, clat : 2 * clat].T,
            wide_mask[:, 2 * clat :].T[:base, :] * high,
        ],
        axis=0,
    )
    skip = lon0 - MARGIN
    for row in range(rows):
        quarter[row] = 0.25 * jnp.broadcast_to(turned[:, row + skip : row + skip + 1], (wide, snaps))

    def coefficients(row, _):
        own = quarter[row]
        keep_lat[row] = 1.0 - (pltpu.roll(own, 1, 0) + pltpu.roll(own, wide - 1, 0))
        even[row] = raw[row] * (4.0 * own)
        return 0

    def coefficients_lon(row, _):
        keep_lon[row] = 1.0 - (quarter[row - 1] + quarter[row + 1])
        return 0

    lax.fori_loop(0, rows, coefficients, 0)
    lax.fori_loop(1, rows - 1, coefficients_lon, 0)

    def sweep(source, target, row):
        scale = quarter[row]
        lon_swept = source[row] * keep_lon[row] + scale * (source[row - 1] + source[row + 1])
        sides = pltpu.roll(lon_swept, 1, 0) + pltpu.roll(lon_swept, wide - 1, 0)
        target[row] = lon_swept * keep_lat[row] + scale * sides

    for step in range(PASSES):
        source, target = (even, odd) if step % 2 == 0 else (odd, even)

        def one_row(row, _, source=source, target=target):
            sweep(source, target, row)
            return 0

        lax.fori_loop(1 + step, rows - 1 - step, one_row, 0)
    field = even if PASSES % 2 == 0 else odd

    def gradients(row, _):
        at = row + MARGIN
        half = 2.0 * quarter[at]
        centre = field[at]
        own = slice(base, base + clat)
        flat[0, row] = centre[own]
        flat[1, row] = (half * (field[at + 1] - field[at - 1]))[own]
        flat[2, row] = (half * (pltpu.roll(centre, wide - 1, 0) - pltpu.roll(centre, 1, 0)))[own]
        return 0

    lax.fori_loop(0, clon, gradients, 0)
    out = pltpu.make_async_copy(flat, flat_ref, out_sem)
    out.start()

    group = 8
    chunks = 3 * clon // group
    per = clon // group

    def gram_chunk(index, total):
        block = flat[lax.div(index, per), pl.ds(lax.rem(index, per) * group, group)]
        block = block.reshape(group * clat, snaps)
        return total + lax.dot_general(
            block, block, (((0,), (0,)), ((), ())), precision=HIGHEST, preferred_element_type=jnp.float32
        )

    gram = lax.fori_loop(0, chunks, gram_chunk, jnp.zeros((snaps, snaps), jnp.float32))
    part[...] = gram.reshape(part.shape)
    all_reduce(place, part, slots_a, slots_b, gram_ref, (sa, ra, sb, rb, sc, rc))
    for copy in copies:
        copy.wait_send()
    out.wait()


def second_kernel(
    n_lon, n_lat,
    flat_ref, inverse_ref, basis_ref, gram_ref,
    basis, part, slots_a, slots_b, sa, ra, sb, rb, sc, rc, out_sem,
):
    place = Place(n_lon, n_lat)
    expected = greet(place, [])
    _, clon, clat, snaps = flat_ref.shape
    group = 8
    chunks = 3 * clon // group
    per = clon // group

    def chunk(index, total):
        which, where = lax.div(index, per), lax.rem(index, per) * group
        block = flat_ref[which, pl.ds(where, group)].reshape(group * clat, snaps)
        turned = lax.dot_general(
            block,
            inverse_ref[...],
            (((1,), (1,)), ((), ())),
            precision=HIGHEST,
            preferred_element_type=jnp.float32,
        )
        basis[which, pl.ds(where, group)] = turned.reshape(group, clat, snaps)
        return total + lax.dot_general(
            turned, turned, (((0,), (0,)), ((), ())), precision=HIGHEST, preferred_element_type=jnp.float32
        )

    gram = lax.fori_loop(0, chunks, chunk, jnp.zeros((snaps, snaps), jnp.float32))
    out = pltpu.make_async_copy(basis, basis_ref, out_sem)
    out.start()
    part[...] = gram.reshape(part.shape)
    pl.semaphore_wait(pltpu.get_barrier_semaphore(), expected)
    all_reduce(place, part, slots_a, slots_b, gram_ref, (sa, ra, sb, rb, sc, rc))
    out.wait()


def last_kernel(scale, basis_ref, inverse_ref, modes_ref):
    _, clon, clat, snaps = basis_ref.shape
    inverse = inverse_ref[...]

    def one(row, _):
        value = lax.dot_general(
            inverse,
            basis_ref[0, row],
            (((1,), (1,)), ((), ())),
            precision=HIGHEST,
            preferred_element_type=jnp.float32,
        )
        modes_ref[:, 0, row, :] = value * scale
        return 0

    lax.fori_loop(0, clon, one, 0, unroll=4)


def whole(memory_space=pltpu.VMEM):
    return pl.BlockSpec(memory_space=memory_space)


def factor(gram):
    lower = jnp.linalg.cholesky(gram)
    eye = jnp.eye(gram.shape[0], dtype=jnp.float32)
    return lower, jax.scipy.linalg.solve_triangular(lower, eye, lower=True)


def on_device(n_lon, n_lat, pressure, ocean_mask):
    snaps, clon, clat = pressure.shape
    size_a = n_lon // Y_LOW
    size_b = n_lat * Y_LOW
    wide, rows = clat + 16, clon + 2 * MARGIN
    f32 = jnp.float32
    limit = 56 * 1024 * 1024
    extended = [pltpu.VMEM((rows, wide, snaps), f32)]
    flat_shape = (3, clon, clat, snaps)
    gram_shape = (size_a, snaps // size_a, snaps)
    flat, gram = pl.pallas_call(
        functools.partial(first_kernel, n_lon, n_lat),
        out_shape=(jax.ShapeDtypeStruct(flat_shape, f32), jax.ShapeDtypeStruct(gram_shape, f32)),
        in_specs=[whole(), whole()],
        out_specs=(whole(pl.ANY), whole()),
        scratch_shapes=extended
        + [pltpu.VMEM((clon + 16, 3 * clat), f32)]
        + 5 * extended
        + [pltpu.VMEM((8, 128), f32), pltpu.VMEM(flat_shape, f32)]
        + reduce_scratch(size_a, size_b, snaps)
        + 4 * [pltpu.SemaphoreType.DMA((len(NEIGHBOURS),))]
        + [pltpu.SemaphoreType.DMA],
        compiler_params=pltpu.CompilerParams(
            collective_id=0, has_side_effects=True, vmem_limit_bytes=limit
        ),
        name="filter_gram",
    )(pressure.reshape(snaps * clon, clat), ocean_mask)
    lower_one, inverse_one = factor(gram.reshape(snaps, snaps))
    basis, gram = pl.pallas_call(
        functools.partial(second_kernel, n_lon, n_lat),
        out_shape=(jax.ShapeDtypeStruct(flat_shape, f32), jax.ShapeDtypeStruct(gram_shape, f32)),
        in_specs=[whole(), whole()],
        out_specs=(whole(pl.ANY), whole()),
        scratch_shapes=[pltpu.VMEM(flat_shape, f32)]
        + reduce_scratch(size_a, size_b, snaps)
        + [pltpu.SemaphoreType.DMA],
        compiler_params=pltpu.CompilerParams(
            collective_id=1, has_side_effects=True, vmem_limit_bytes=limit
        ),
        name="basis_gram",
    )(flat, inverse_one)
    lower_two, inverse_two = factor(gram.reshape(snaps, snaps))
    total_rows = 3 * clon * clat * n_lon * n_lat
    scale = float(total_rows) ** 0.5
    modes = pl.pallas_call(
        functools.partial(last_kernel, scale),
        grid=(3,),
        out_shape=jax.ShapeDtypeStruct((snaps, 3, clon, clat), f32),
        in_specs=[pl.BlockSpec((1, clon, clat, snaps), lambda i: (i, 0, 0, 0)), whole()],
        out_specs=pl.BlockSpec((snaps, 1, clon, clat), lambda i: (0, i, 0, 0)),
        compiler_params=pltpu.CompilerParams(vmem_limit_bytes=32 * 1024 * 1024),
        name="modes",
    )(basis, inverse_two)
    factor_r = (
        jnp.dot(lower_two.T, lower_one.T, precision=HIGHEST, preferred_element_type=f32) / scale
    )
    return (modes, factor_r)


def solution(mesh):
    n_lon, n_lat = mesh.shape["lon"], mesh.shape["lat"]
    return jax.shard_map(
        functools.partial(on_device, n_lon, n_lat),
        mesh=mesh,
        in_specs=(P(None, "lon", "lat"), P("lon", "lat")),
        out_specs=(P(None, None, "lon", "lat"), P()),
        check_vma=False,
    )
```

```python
import functools

import jax
import jax.numpy as jnp
from jax import lax
from jax.experimental import pallas as pl
from jax.experimental.pallas import tpu as pltpu
from jax.sharding import PartitionSpec as P

PASSES = 4
MARGIN = PASSES + 1
CORES = 2
Y_LOW = 4
Y_HIGH = 2
BLOCK = 16
BASE = 8
MESH = pl.DeviceIdType.MESH
HIGHEST = lax.Precision.HIGHEST
F32, BF16 = jnp.float32, jnp.bfloat16


def steps_of(size):
    return sorted(range(1, size), key=lambda step: -min(step, size - step))


class Place:
    def __init__(self, n_lon, n_lat):
        self.n_lon, self.n_lat = n_lon, n_lat
        self.n_z = n_lon // (Y_LOW * CORES)
        self.n_y = Y_LOW * Y_HIGH
        self.n_x = n_lat // Y_HIGH
        self.n_a = self.n_x * CORES
        self.lon = lax.axis_index("lon")
        self.lat = lax.axis_index("lat")
        pair = lax.div(self.lon, CORES)
        self.core = lax.rem(self.lon, CORES)
        self.z = lax.div(pair, Y_LOW)
        self.x = lax.div(self.lat, Y_HIGH)
        self.y = lax.rem(self.lat, Y_HIGH) * Y_LOW + lax.rem(pair, Y_LOW)
        self.a = self.x * CORES + self.core

    def device(self, x, y, z, core):
        lon = (z * Y_LOW + lax.rem(y, Y_LOW)) * CORES + core
        return lon, x * Y_HIGH + lax.div(y, Y_LOW)

    def peer_a(self, step):
        rank = lax.rem(self.a + step, self.n_a)
        return rank, self.device(lax.div(rank, CORES), self.y, self.z, lax.rem(rank, CORES))

    def peer_y(self, step):
        rank = lax.rem(self.y + step, self.n_y)
        return rank, self.device(self.x, rank, self.z, self.core)

    def peer_z(self, step):
        rank = lax.rem(self.z + step, self.n_z)
        return rank, self.device(self.x, self.y, rank, self.core)

    def near(self, dlon, dlat):
        return (
            lax.rem(self.lon + dlon + self.n_lon, self.n_lon),
            lax.rem(self.lat + dlat + self.n_lat, self.n_lat),
        )

    def reduce_peers(self):
        groups = ((self.peer_a, self.n_a), (self.peer_y, self.n_y), (self.peer_z, self.n_z))
        return [peer(step)[1] for peer, size in groups for step in steps_of(size)]


def greet(devices):
    barrier = pltpu.get_barrier_semaphore()
    for device in devices:
        pl.semaphore_signal(barrier, inc=1, device_id=device, device_id_type=MESH)
    return len(devices)


def send(src, dst, send_sem, recv_sem, device):
    return pltpu.make_async_remote_copy(
        src_ref=src,
        dst_ref=dst,
        send_sem=send_sem,
        recv_sem=recv_sem,
        device_id=device,
        device_id_type=MESH,
    )


def exchange(peer, size, mine, source, target, sends, recvs):
    ranks = [peer(step) for step in steps_of(size)]
    started = [
        send(source(rank), target.at[mine], sends.at[rank], recvs.at[mine], device)
        for rank, device in ranks
    ]
    for copy in started:
        copy.start()

    def arrived():
        for rank, device in ranks:
            send(source(rank), target.at[rank], sends.at[rank], recvs.at[rank], device).wait_recv()

    def sent():
        for copy in started:
            copy.wait_send()

    return arrived, sent


def all_reduce(place, part, slots_a, slots_y, slots_z, total, sems):
    a, y, z = place.a, place.y, place.z
    arrived, sent_a = exchange(
        place.peer_a, place.n_a, a, lambda rank: part.at[rank], slots_a, sems[0], sems[1]
    )
    slots_a[a] = part[a]
    arrived()
    slots_y[y] = jnp.sum(slots_a[...], axis=0)
    arrived, sent_y = exchange(
        place.peer_y, place.n_y, y, lambda _: slots_y.at[y], slots_y, sems[2], sems[3]
    )
    arrived()
    slots_z[z] = jnp.sum(slots_y[...], axis=0)
    arrived, sent_z = exchange(
        place.peer_z, place.n_z, z, lambda _: slots_z.at[z], slots_z, sems[4], sems[5]
    )
    arrived()
    total[a] = jnp.sum(slots_z[...], axis=0)
    arrived, sent_b = exchange(
        place.peer_a, place.n_a, a, lambda _: total.at[a], total, sems[6], sems[7]
    )
    arrived()
    for sent in (sent_a, sent_y, sent_z, sent_b):
        sent()


def group_sizes(n_lon, n_lat):
    return n_lat // Y_HIGH * CORES, Y_LOW * Y_HIGH, n_lon // (Y_LOW * CORES)


def reduce_scratch(n_lon, n_lat, snaps):
    n_a, n_y, n_z = group_sizes(n_lon, n_lat)
    piece = (snaps // n_a, snaps)
    slots = [pltpu.VMEM((size, *piece), F32) for size in (n_a, n_a, n_y, n_z)]
    return slots + [pltpu.SemaphoreType.DMA((size,)) for size in (n_a, n_y, n_z, n_a) for _ in (0, 1)]


def split(value):
    one = value.astype(BF16)
    rest = value - one.astype(F32)
    two = rest.astype(BF16)
    return one, two, (rest - two.astype(F32)).astype(BF16)


def multiply(left, right, left_dim, right_dim):
    return lax.dot_general(
        left, right, (((left_dim,), (right_dim,)), ((), ())), preferred_element_type=F32
    )


def exact_dot(left, right, left_dim, right_dim):
    return lax.dot_general(
        left,
        right,
        (((left_dim,), (right_dim,)), ((), ())),
        precision=HIGHEST,
        preferred_element_type=F32,
    )


def set_weights(matrix, wide, narrow):
    one, two, three = split(matrix)
    pair = jnp.concatenate([one, two], axis=1)
    wide[...] = jnp.concatenate([pair, pair], axis=0)
    narrow[...] = jnp.concatenate([three, one], axis=0)


def apply_weights(value, wide, narrow):
    columns = value.shape[1]
    one, two, three = split(value)
    main = multiply(jnp.concatenate([one, two], axis=1), wide[...], 1, 0)
    rest = multiply(jnp.concatenate([one, three], axis=1), narrow[...], 1, 0)
    return main[:, :columns] + (main[:, columns:] + rest)


def gram_parts(value):
    one, two, three = split(value)
    pair = jnp.concatenate([one, two], axis=1)
    return multiply(pair, pair, 0, 0), multiply(one, three, 0, 0)


def gram_start(columns):
    return jnp.zeros((2 * columns, 2 * columns), F32), jnp.zeros((columns, columns), F32)


def gram_end(main, side):
    n = side.shape[0]
    cross = main[n:, :n] + main[:n, n:] + (main[n:, n:] + (side + side.T))
    return main[:n, :n] + cross


def span(delta, own_at, own, margin):
    if delta == 0:
        return pl.ds(own_at, own), pl.ds(own_at, own)
    if delta > 0:
        return pl.ds(own_at + own - margin, margin), pl.ds(own_at - margin, margin)
    return pl.ds(own_at, margin), pl.ds(own_at + own, margin)


def first_kernel(
    n_lon, n_lat,
    p_hbm, mask_ref, flat, gram_ref,
    p_ref, raw, masks, even, odd, quarter, keep_lon, keep_lat,
    part, slots_a, slots_y, slots_z, *sems,
):
    reduce_sems, (near_send, near_recv, load_sem) = sems[:8], sems[8:]
    place = Place(n_lon, n_lat)
    clon, clat = mask_ref.shape
    snaps = raw.shape[2]
    wide = clat + 2 * BASE
    rows = clon + 2 * MARGIN
    load = pltpu.make_async_copy(p_hbm, p_ref, load_sem)
    load.start()
    sides = [place.near(0, 1), place.near(0, -1), place.near(1, 0), place.near(-1, 0)]
    expected = greet(sides + place.reduce_peers())

    own_lon, own_lat = pl.ds(BASE, clon), pl.ds(clat, clat)
    masks[own_lon, own_lat] = mask_ref[...].astype(F32)
    load.wait()

    def turn(row):
        raw[MARGIN + row, BASE : BASE + clat, :] = p_ref[pl.ds(row, snaps, stride=clon), :].T

    for row in range(clon):
        turn(row)

    pl.semaphore_wait(pltpu.get_barrier_semaphore(), expected)

    def near(index, source, target, device):
        return send(source, target, near_send.at[index], near_recv.at[index], device)

    lat_mask, lat_field, lon_mask, lon_field, corners = [], [], [], [], []
    for index, delta in enumerate((1, -1)):
        device = place.near(0, delta)
        src, dst = span(delta, clat, clat, clat)
        lat_mask.append(
            near(index, masks.at[own_lon, own_lat], masks.at[own_lon, dst], device)
        )
        src, dst = span(delta, BASE, clat, MARGIN)
        inner = pl.ds(MARGIN, clon)
        lat_field.append(near(2 + index, raw.at[inner, src, :], raw.at[inner, dst, :], device))
    for index, delta in enumerate((1, -1)):
        device = place.near(delta, 0)
        src, dst = span(delta, BASE, clon, MARGIN)
        lon_mask.append(near(4 + index, masks.at[src, :], masks.at[dst, :], device))
        src, dst = span(delta, MARGIN, clon, MARGIN)
        inner = pl.ds(BASE, clat)
        lon_field.append(near(6 + index, raw.at[src, inner, :], raw.at[dst, inner, :], device))
        for end, at in enumerate((BASE - MARGIN, BASE + clat)):
            outer = pl.ds(at, MARGIN)
            number = 8 + 2 * index + end
            corners.append(near(number, raw.at[src, outer, :], raw.at[dst, outer, :], device))
    for copy in lat_mask + lat_field + lon_field:
        copy.start()
    for copy in lat_mask:
        copy.wait_recv()
    for copy in lon_mask:
        copy.start()
    for copy in lat_field:
        copy.wait_recv()
    for copy in corners:
        copy.start()
    for copy in lon_mask:
        copy.wait_recv()

    low = jnp.where(place.lat > 0, 1.0, 0.0)
    high = jnp.where(place.lat < n_lat - 1, 1.0, 0.0)
    turned = jnp.concatenate(
        [
            masks[:, 0:clat].T[clat - BASE :, :] * low,
            masks[:, clat : 2 * clat].T,
            masks[:, 2 * clat :].T[:BASE, :] * high,
        ],
        axis=0,
    )
    skip = BASE - MARGIN
    for row in range(rows):
        quarter[row] = 0.25 * jnp.broadcast_to(turned[:, row + skip : row + skip + 1], (wide, snaps))

    def coefficients(row, _):
        own = quarter[row]
        keep_lat[row] = 1.0 - (pltpu.roll(own, 1, 0) + pltpu.roll(own, wide - 1, 0))
        keep_lon[row] = 1.0 - (quarter[row - 1] + quarter[row + 1])
        return 0

    lax.fori_loop(1, rows - 1, coefficients, 0)
    for copy in lon_field + corners:
        copy.wait_recv()

    def masked(row, _):
        even[row] = raw[row] * (4.0 * quarter[row])
        return 0

    lax.fori_loop(0, rows, masked, 0)

    def sweep(source, target, row):
        scale = quarter[row]
        lon_swept = source[row] * keep_lon[row] + scale * (source[row - 1] + source[row + 1])
        both = pltpu.roll(lon_swept, 1, 0) + pltpu.roll(lon_swept, wide - 1, 0)
        target[row] = lon_swept * keep_lat[row] + scale * both

    for step in range(PASSES):
        source, target = (even, odd) if step % 2 == 0 else (odd, even)

        def one_row(row, _, source=source, target=target):
            sweep(source, target, row)
            return 0

        lax.fori_loop(1 + step, rows - 1 - step, one_row, 0)
    field = even if PASSES % 2 == 0 else odd

    def gradients(row, _):
        at = row + MARGIN
        half = 2.0 * quarter[at]
        centre = field[at]
        own = slice(BASE, BASE + clat)
        flat[0, row] = centre[own]
        flat[1, row] = (half * (field[at + 1] - field[at - 1]))[own]
        flat[2, row] = (half * (pltpu.roll(centre, wide - 1, 0) - pltpu.roll(centre, 1, 0)))[own]
        return 0

    lax.fori_loop(0, clon, gradients, 0)

    def gram_chunk(which, carry):
        main, side = gram_parts(flat[which].reshape(clon * clat, snaps))
        return carry[0] + main, carry[1] + side

    gram = gram_end(*lax.fori_loop(0, 3, gram_chunk, gram_start(snaps)))
    part[...] = gram.reshape(part.shape)
    all_reduce(place, part, slots_a, slots_y, slots_z, gram_ref, reduce_sems)
    for copy in lat_mask + lat_field + lon_mask + lon_field + corners:
        copy.wait_send()


def second_kernel(
    n_lon, n_lat,
    flat_ref, inverse_ref, basis, gram_ref,
    wide, narrow, part, slots_a, slots_y, slots_z, *sems,
):
    place = Place(n_lon, n_lat)
    expected = greet(place.reduce_peers())
    _, clon, clat, snaps = flat_ref.shape
    group = 8
    per = clon // group
    set_weights(inverse_ref[...].T, wide, narrow)

    def chunk(index, carry):
        which, where = lax.div(index, per), lax.rem(index, per) * group
        value = flat_ref[which, pl.ds(where, group)].reshape(group * clat, snaps)
        value = apply_weights(value, wide, narrow)
        basis[which, pl.ds(where, group)] = value.reshape(group, clat, snaps)
        main, side = gram_parts(value)
        return carry[0] + main, carry[1] + side

    gram = gram_end(*lax.fori_loop(0, 3 * per, chunk, gram_start(snaps)))
    part[...] = gram.reshape(part.shape)
    pl.semaphore_wait(pltpu.get_barrier_semaphore(), expected)
    all_reduce(place, part, slots_a, slots_y, slots_z, gram_ref, sems)


def factorize(gram, left_work, right_work, panel, spread, upper_ref, inverse_ref):
    n = gram.shape[0]
    rows = lax.broadcasted_iota(jnp.int32, (n, n), 0)
    columns = lax.broadcasted_iota(jnp.int32, (n, n), 1)
    left_work[...] = gram
    right_work[...] = jnp.where(rows == columns, 1.0, 0.0)
    for at in range(0, n, BLOCK):
        for j in range(BLOCK):
            column = left_work[at : at + BLOCK, at + j : at + j + 1]
            spread[j] = jnp.broadcast_to(column, (BLOCK, n))

        def row_of(ref, i):
            return jnp.broadcast_to(ref[i : i + 1, :], (8, n))

        scalar = {
            (i, j): row_of(spread.at[j], i) for j in range(BLOCK) for i in range(j, BLOCK)
        }
        left = [row_of(left_work, at + i) for i in range(BLOCK)]
        right = [row_of(right_work, at + i) for i in range(BLOCK)]
        for j in range(BLOCK):
            pivot = scalar[j, j]
            root = lax.rsqrt(pivot)
            root = root * (1.5 - 0.5 * pivot * root * root)
            below = {i: scalar[i, j] * root for i in range(j + 1, BLOCK)}
            left[j] = left[j] * root
            right[j] = right[j] * root
            for i in range(j + 1, BLOCK):
                for k in range(j + 1, i + 1):
                    scalar[i, k] = scalar[i, k] - below[i] * below[k]
                left[i] = left[i] - below[i] * left[j]
                right[i] = right[i] - below[i] * right[j]
        for j in range(BLOCK):
            panel[j : j + 1, :n] = left[j][:1]
            panel[j : j + 1, n:] = right[j][:1]
        done = at + BLOCK
        upper_ref[at:done, :] = panel[:, :n]
        inverse_ref[at:done, :] = panel[:, n:]
        for low, high in ((done, done + BLOCK), (done + BLOCK, n)):
            if low < high <= n:
                change = exact_dot(panel[:, low:high], panel[...], 0, 0)
                left_work[low:high, :] = left_work[low:high, :] - change[:, :n]
                right_work[low:high, :] = right_work[low:high, :] - change[:, n:]
    upper_ref[...] = jnp.where(columns >= rows, upper_ref[...], 0.0)


def factor_scratch(n):
    return [
        pltpu.VMEM((n, n), F32),
        pltpu.VMEM((n, n), F32),
        pltpu.VMEM((BLOCK, 2 * n), F32),
        pltpu.VMEM((BLOCK, BLOCK, n), F32),
    ]


def factor_kernel(gram_ref, upper_ref, inverse_ref, *work):
    factorize(gram_ref[...].reshape(upper_ref.shape), *work, upper_ref, inverse_ref)


def last_kernel(
    scale,
    basis, gram_ref, first_upper, modes_ref, factor_ref,
    upper, inverse, wide, narrow, staged, out_sem, *work,
):
    _, clon, clat, snaps = basis.shape
    factorize(gram_ref[...].reshape(upper.shape), *work, upper, inverse)
    set_weights(inverse[...].T * scale, wide, narrow)
    group = 8
    copies = []
    for which in range(3):
        for part in range(clon // group):
            start = part * group
            value = basis[which, start : start + group].reshape(group * clat, snaps)
            value = apply_weights(value, wide, narrow)
            for row in range(group):
                staged[:, which, start + row, :] = value[row * clat : (row + 1) * clat].T
            here = (slice(None), which, pl.ds(start, group), slice(None))
            copy = pltpu.make_async_copy(staged.at[here], modes_ref.at[here], out_sem.at[len(copies)])
            copy.start()
            copies.append(copy)
    factor_ref[...] = exact_dot(upper[...], first_upper[...], 1, 0) * (1.0 / scale)
    for copy in copies:
        copy.wait()


def whole(memory_space=pltpu.VMEM):
    return pl.BlockSpec(memory_space=memory_space)


def on_device(n_lon, n_lat, pressure, ocean_mask):
    snaps, clon, clat = pressure.shape
    n_a, _, _ = group_sizes(n_lon, n_lat)
    rows, wide = clon + 2 * MARGIN, clat + 2 * BASE
    mib = 1024 * 1024
    flat = jax.ShapeDtypeStruct((3, clon, clat, snaps), F32)
    pieces = jax.ShapeDtypeStruct((n_a, snaps // n_a, snaps), F32)
    square = jax.ShapeDtypeStruct((snaps, snaps), F32)
    weights = [pltpu.VMEM((2 * snaps, 2 * snaps), BF16), pltpu.VMEM((2 * snaps, snaps), BF16)]
    extended = pltpu.VMEM((rows, wide, snaps), F32)

    def params(limit, collective_id=None):
        more = {} if collective_id is None else {"collective_id": collective_id, "has_side_effects": True}
        return pltpu.CompilerParams(vmem_limit_bytes=limit * mib, **more)

    field, gram = pl.pallas_call(
        functools.partial(first_kernel, n_lon, n_lat),
        out_shape=(flat, pieces),
        in_specs=[whole(pltpu.HBM), whole()],
        out_specs=(whole(), whole()),
        scratch_shapes=[pltpu.VMEM((snaps * clon, clat), F32), extended]
        + [pltpu.VMEM((clon + 2 * BASE, 3 * clat), F32)]
        + 5 * [extended]
        + reduce_scratch(n_lon, n_lat, snaps)
        + 2 * [pltpu.SemaphoreType.DMA((12,))]
        + [pltpu.SemaphoreType.DMA],
        compiler_params=params(32, 0),
        name="filter_gram",
    )(
        pltpu.with_memory_space_constraint(pressure.reshape(snaps * clon, clat), pltpu.HBM), ocean_mask
    )
    first_upper, first_inverse = pl.pallas_call(
        factor_kernel,
        out_shape=(square, square),
        in_specs=[whole()],
        out_specs=(whole(), whole()),
        scratch_shapes=factor_scratch(snaps),
        compiler_params=params(8),
        name="factor",
    )(gram)
    basis, gram = pl.pallas_call(
        functools.partial(second_kernel, n_lon, n_lat),
        out_shape=(flat, pieces),
        in_specs=[whole(), whole()],
        out_specs=(whole(), whole()),
        scratch_shapes=weights + reduce_scratch(n_lon, n_lat, snaps),
        compiler_params=params(20, 1),
        name="basis_gram",
    )(field, first_inverse)
    scale = float(3 * clon * clat * n_lon * n_lat) ** 0.5
    return pl.pallas_call(
        functools.partial(last_kernel, scale),
        out_shape=(jax.ShapeDtypeStruct((snaps, 3, clon, clat), F32), square),
        in_specs=[whole(), whole(), whole()],
        out_specs=(whole(pltpu.HBM), whole()),
        scratch_shapes=[pltpu.VMEM((snaps, snaps), F32)] * 2
        + weights
        + [pltpu.VMEM((snaps, 3, clon, clat), F32), pltpu.SemaphoreType.DMA((6,))]
        + factor_scratch(snaps),
        compiler_params=params(24),
        name="factor_modes",
    )(basis, gram, first_upper)


def solution(mesh):
    n_lon, n_lat = mesh.shape["lon"], mesh.shape["lat"]
    return jax.shard_map(
        functools.partial(on_device, n_lon, n_lat),
        mesh=mesh,
        in_specs=(P(None, "lon", "lat"), P("lon", "lat")),
        out_specs=(P(None, None, "lon", "lat"), P()),
        check_vma=False,
    )
```

```python
import functools

import jax
import jax.numpy as jnp
from jax import lax
from jax.experimental import pallas as pl
from jax.experimental.pallas import tpu as pltpu
from jax.sharding import PartitionSpec as P

PASSES = 4
MARGIN = PASSES + 1
CORES = 2
Y_LOW = 4
Y_HIGH = 2
BLOCK = 16
BASE = 8
MESH = pl.DeviceIdType.MESH
HIGHEST = lax.Precision.HIGHEST
F32, BF16 = jnp.float32, jnp.bfloat16


def steps_of(size):
    return sorted(range(1, size), key=lambda step: -min(step, size - step))


class Place:
    def __init__(self, n_lon, n_lat):
        self.n_lon, self.n_lat = n_lon, n_lat
        self.n_z = n_lon // (Y_LOW * CORES)
        self.n_y = Y_LOW * Y_HIGH
        self.n_x = n_lat // Y_HIGH
        self.n_a = self.n_x * CORES
        self.lon = lax.axis_index("lon")
        self.lat = lax.axis_index("lat")
        pair = lax.div(self.lon, CORES)
        self.core = lax.rem(self.lon, CORES)
        self.z = lax.div(pair, Y_LOW)
        self.x = lax.div(self.lat, Y_HIGH)
        self.y = lax.rem(self.lat, Y_HIGH) * Y_LOW + lax.rem(pair, Y_LOW)
        self.a = self.x * CORES + self.core

    def device(self, x, y, z, core):
        lon = (z * Y_LOW + lax.rem(y, Y_LOW)) * CORES + core
        return lon, x * Y_HIGH + lax.div(y, Y_LOW)

    def peer_a(self, step):
        rank = lax.rem(self.a + step, self.n_a)
        return rank, self.device(lax.div(rank, CORES), self.y, self.z, lax.rem(rank, CORES))

    def peer_y(self, step):
        rank = lax.rem(self.y + step, self.n_y)
        return rank, self.device(self.x, rank, self.z, self.core)

    def peer_z(self, step):
        rank = lax.rem(self.z + step, self.n_z)
        return rank, self.device(self.x, self.y, rank, self.core)

    def near(self, dlon, dlat):
        return (
            lax.rem(self.lon + dlon + self.n_lon, self.n_lon),
            lax.rem(self.lat + dlat + self.n_lat, self.n_lat),
        )

    def reduce_peers(self):
        groups = ((self.peer_a, self.n_a), (self.peer_y, self.n_y), (self.peer_z, self.n_z))
        return [peer(step)[1] for peer, size in groups for step in steps_of(size)]


def greet(devices):
    barrier = pltpu.get_barrier_semaphore()
    for device in devices:
        pl.semaphore_signal(barrier, inc=1, device_id=device, device_id_type=MESH)
    return len(devices)


def send(src, dst, send_sem, recv_sem, device):
    return pltpu.make_async_remote_copy(
        src_ref=src,
        dst_ref=dst,
        send_sem=send_sem,
        recv_sem=recv_sem,
        device_id=device,
        device_id_type=MESH,
    )


def exchange(peer, size, mine, source, target, sends, recvs):
    ranks = [peer(step) for step in steps_of(size)]
    started = [
        send(source(rank), target.at[mine], sends.at[rank], recvs.at[mine], device)
        for rank, device in ranks
    ]
    for copy in started:
        copy.start()

    def arrived():
        for rank, device in ranks:
            send(source(rank), target.at[rank], sends.at[rank], recvs.at[rank], device).wait_recv()

    def sent():
        for copy in started:
            copy.wait_send()

    return arrived, sent


def all_reduce(place, part, slots_a, slots_y, slots_z, total, sems):
    a, y, z = place.a, place.y, place.z
    arrived, sent_a = exchange(
        place.peer_a, place.n_a, a, lambda rank: part.at[rank], slots_a, sems[0], sems[1]
    )
    slots_a[a] = part[a]
    arrived()
    slots_y[y] = jnp.sum(slots_a[...], axis=0)
    arrived, sent_y = exchange(
        place.peer_y, place.n_y, y, lambda _: slots_y.at[y], slots_y, sems[2], sems[3]
    )
    arrived()
    slots_z[z] = jnp.sum(slots_y[...], axis=0)
    arrived, sent_z = exchange(
        place.peer_z, place.n_z, z, lambda _: slots_z.at[z], slots_z, sems[4], sems[5]
    )
    arrived()
    total[a] = jnp.sum(slots_z[...], axis=0)
    arrived, sent_b = exchange(
        place.peer_a, place.n_a, a, lambda _: total.at[a], total, sems[6], sems[7]
    )
    arrived()
    for sent in (sent_a, sent_y, sent_z, sent_b):
        sent()


def group_sizes(n_lon, n_lat):
    return n_lat // Y_HIGH * CORES, Y_LOW * Y_HIGH, n_lon // (Y_LOW * CORES)


def reduce_scratch(n_lon, n_lat, snaps):
    n_a, n_y, n_z = group_sizes(n_lon, n_lat)
    piece = (snaps // n_a, snaps)
    slots = [pltpu.VMEM((size, *piece), F32) for size in (n_a, n_a, n_y, n_z)]
    return slots + [pltpu.SemaphoreType.DMA((size,)) for size in (n_a, n_y, n_z, n_a) for _ in (0, 1)]


def split(value):
    one = value.astype(BF16)
    rest = value - one.astype(F32)
    two = rest.astype(BF16)
    return one, two, (rest - two.astype(F32)).astype(BF16)


def multiply(left, right, left_dim, right_dim):
    return lax.dot_general(
        left, right, (((left_dim,), (right_dim,)), ((), ())), preferred_element_type=F32
    )


def exact_dot(left, right, left_dim, right_dim):
    return lax.dot_general(
        left,
        right,
        (((left_dim,), (right_dim,)), ((), ())),
        precision=HIGHEST,
        preferred_element_type=F32,
    )


def set_weights(matrix, wide, narrow):
    one, two, three = split(matrix)
    pair = jnp.concatenate([one, two], axis=1)
    wide[...] = jnp.concatenate([pair, pair], axis=0)
    narrow[...] = jnp.concatenate([three, one], axis=0)


def apply_weights(value, wide, narrow):
    columns = value.shape[1]
    one, two, three = split(value)
    main = multiply(jnp.concatenate([one, two], axis=1), wide[...], 1, 0)
    rest = multiply(jnp.concatenate([one, three], axis=1), narrow[...], 1, 0)
    return main[:, :columns] + (main[:, columns:] + rest)


def gram_parts(value):
    one, two, three = split(value)
    pair = jnp.concatenate([one, two], axis=1)
    return multiply(pair, pair, 0, 0), multiply(one, three, 0, 0)


def gram_start(columns):
    return jnp.zeros((2 * columns, 2 * columns), F32), jnp.zeros((columns, columns), F32)


def gram_end(main, side):
    n = side.shape[0]
    cross = main[n:, :n] + main[:n, n:] + (main[n:, n:] + (side + side.T))
    return main[:n, :n] + cross


def span(delta, own_at, own, margin):
    if delta == 0:
        return pl.ds(own_at, own), pl.ds(own_at, own)
    if delta > 0:
        return pl.ds(own_at + own - margin, margin), pl.ds(own_at - margin, margin)
    return pl.ds(own_at, margin), pl.ds(own_at + own, margin)


def first_kernel(
    n_lon, n_lat,
    p_hbm, mask_hbm, flat, gram_ref,
    p_ref, mask_ref, raw, masks, even, odd, quarter, keep_lon, keep_lat,
    part, slots_a, slots_y, slots_z, *sems,
):
    reduce_sems, (near_send, near_recv, load_sem, mask_sem) = sems[:8], sems[8:]
    place = Place(n_lon, n_lat)
    clon, clat = mask_ref.shape
    snaps = raw.shape[2]
    wide = clat + 2 * BASE
    rows = clon + 2 * MARGIN
    load = pltpu.make_async_copy(p_hbm, p_ref, load_sem)
    load.start()
    load_mask = pltpu.make_async_copy(mask_hbm, mask_ref, mask_sem)
    load_mask.start()
    sides = [place.near(0, 1), place.near(0, -1), place.near(1, 0), place.near(-1, 0)]
    expected = greet(sides + place.reduce_peers())

    own_lon, own_lat = pl.ds(BASE, clon), pl.ds(clat, clat)
    load_mask.wait()
    masks[own_lon, own_lat] = mask_ref[...].astype(F32)
    load.wait()

    def turn(row):
        raw[MARGIN + row, BASE : BASE + clat, :] = p_ref[pl.ds(row, snaps, stride=clon), :].T

    for row in range(clon):
        turn(row)

    pl.semaphore_wait(pltpu.get_barrier_semaphore(), expected)

    def near(index, source, target, device):
        return send(source, target, near_send.at[index], near_recv.at[index], device)

    lat_mask, lat_field, lon_mask, lon_field, corners = [], [], [], [], []
    for index, delta in enumerate((1, -1)):
        device = place.near(0, delta)
        src, dst = span(delta, clat, clat, clat)
        lat_mask.append(
            near(index, masks.at[own_lon, own_lat], masks.at[own_lon, dst], device)
        )
        src, dst = span(delta, BASE, clat, MARGIN)
        inner = pl.ds(MARGIN, clon)
        lat_field.append(near(2 + index, raw.at[inner, src, :], raw.at[inner, dst, :], device))
    for index, delta in enumerate((1, -1)):
        device = place.near(delta, 0)
        src, dst = span(delta, BASE, clon, MARGIN)
        lon_mask.append(near(4 + index, masks.at[src, :], masks.at[dst, :], device))
        src, dst = span(delta, MARGIN, clon, MARGIN)
        inner = pl.ds(BASE, clat)
        lon_field.append(near(6 + index, raw.at[src, inner, :], raw.at[dst, inner, :], device))
        for end, at in enumerate((BASE - MARGIN, BASE + clat)):
            outer = pl.ds(at, MARGIN)
            number = 8 + 2 * index + end
            corners.append(near(number, raw.at[src, outer, :], raw.at[dst, outer, :], device))
    for copy in lat_mask + lat_field:
        copy.start()
    for copy in lat_field:
        copy.wait_send()
    for copy in lon_field:
        copy.start()
    for copy in lat_mask:
        copy.wait_recv()
    for copy in lon_mask:
        copy.start()
    for copy in lat_field:
        copy.wait_recv()
    for copy in corners:
        copy.start()
    for copy in lon_mask:
        copy.wait_recv()

    low = jnp.where(place.lat > 0, 1.0, 0.0)
    high = jnp.where(place.lat < n_lat - 1, 1.0, 0.0)
    turned = jnp.concatenate(
        [
            masks[:, 0:clat].T[clat - BASE :, :] * low,
            masks[:, clat : 2 * clat].T,
            masks[:, 2 * clat :].T[:BASE, :] * high,
        ],
        axis=0,
    )
    skip = BASE - MARGIN
    for row in range(rows):
        quarter[row] = 0.25 * jnp.broadcast_to(turned[:, row + skip : row + skip + 1], (wide, snaps))

    def coefficients(row, _):
        own = quarter[row]
        keep_lat[row] = 1.0 - (pltpu.roll(own, 1, 0) + pltpu.roll(own, wide - 1, 0))
        keep_lon[row] = 1.0 - (quarter[row - 1] + quarter[row + 1])
        return 0

    lax.fori_loop(1, rows - 1, coefficients, 0)

    def masked(row, _):
        even[row] = raw[row] * (4.0 * quarter[row])
        return 0

    def sweep(source, target, row):
        scale = quarter[row]
        lon_swept = source[row] * keep_lon[row] + scale * (source[row - 1] + source[row + 1])
        both = pltpu.roll(lon_swept, 1, 0) + pltpu.roll(lon_swept, wide - 1, 0)
        target[row] = lon_swept * keep_lat[row] + scale * both

    buffers = [(even, odd) if step % 2 == 0 else (odd, even) for step in range(PASSES)]
    first, last = MARGIN, MARGIN + clon
    lax.fori_loop(first, last, masked, 0)
    for step, (source, target) in enumerate(buffers):

        def inner_row(row, _, source=source, target=target):
            sweep(source, target, row)
            return 0

        lax.fori_loop(first + 1 + step, last - 1 - step, inner_row, 0)
    for copy in lon_field + corners:
        copy.wait_recv()
    lax.fori_loop(0, first, masked, 0)
    lax.fori_loop(last, rows, masked, 0)
    for step, (source, target) in enumerate(buffers):

        def outer_rows(row, _, source=source, target=target, step=step):
            sweep(source, target, 1 + step + row)
            sweep(source, target, last - 1 - step + row)
            return 0

        lax.fori_loop(0, MARGIN, outer_rows, 0)
    field = even if PASSES % 2 == 0 else odd

    def gradients(row, _):
        at = row + MARGIN
        half = 2.0 * quarter[at]
        centre = field[at]
        own = slice(BASE, BASE + clat)
        flat[0, row] = centre[own]
        flat[1, row] = (half * (field[at + 1] - field[at - 1]))[own]
        flat[2, row] = (half * (pltpu.roll(centre, wide - 1, 0) - pltpu.roll(centre, 1, 0)))[own]
        return 0

    lax.fori_loop(0, clon, gradients, 0)

    def gram_chunk(which, carry):
        main, side = gram_parts(flat[which].reshape(clon * clat, snaps))
        return carry[0] + main, carry[1] + side

    gram = gram_end(*lax.fori_loop(0, 3, gram_chunk, gram_start(snaps)))
    part[...] = gram.reshape(part.shape)
    all_reduce(place, part, slots_a, slots_y, slots_z, gram_ref, reduce_sems)
    for copy in lat_mask + lon_mask + lon_field + corners:
        copy.wait_send()


def second_kernel(
    n_lon, n_lat,
    flat_ref, inverse_ref, basis, gram_ref,
    wide, narrow, part, slots_a, slots_y, slots_z, *sems,
):
    place = Place(n_lon, n_lat)
    expected = greet(place.reduce_peers())
    _, clon, clat, snaps = flat_ref.shape
    group = 8
    per = clon // group
    set_weights(inverse_ref[...].T, wide, narrow)

    def chunk(index, carry):
        which, where = lax.div(index, per), lax.rem(index, per) * group
        value = flat_ref[which, pl.ds(where, group)].reshape(group * clat, snaps)
        value = apply_weights(value, wide, narrow)
        basis[which, pl.ds(where, group)] = value.reshape(group, clat, snaps)
        main, side = gram_parts(value)
        return carry[0] + main, carry[1] + side

    gram = gram_end(*lax.fori_loop(0, 3 * per, chunk, gram_start(snaps)))
    part[...] = gram.reshape(part.shape)
    pl.semaphore_wait(pltpu.get_barrier_semaphore(), expected)
    all_reduce(place, part, slots_a, slots_y, slots_z, gram_ref, sems)


def factorize(gram, left_work, right_work, panel, spread, upper_ref, inverse_ref):
    n = gram.shape[0]
    rows = lax.broadcasted_iota(jnp.int32, (n, n), 0)
    columns = lax.broadcasted_iota(jnp.int32, (n, n), 1)
    left_work[...] = gram
    right_work[...] = jnp.where(rows == columns, 1.0, 0.0)
    for at in range(0, n, BLOCK):
        for j in range(BLOCK):
            column = left_work[at : at + BLOCK, at + j : at + j + 1]
            spread[j] = jnp.broadcast_to(column, (BLOCK, n))

        def row_of(ref, i):
            return jnp.broadcast_to(ref[i : i + 1, :], (8, n))

        scalar = {
            (i, j): row_of(spread.at[j], i) for j in range(BLOCK) for i in range(j, BLOCK)
        }
        left = [row_of(left_work, at + i) for i in range(BLOCK)]
        right = [row_of(right_work, at + i) for i in range(BLOCK)]
        for j in range(BLOCK):
            root = lax.rsqrt(scalar[j, j])
            below = {i: scalar[i, j] * root for i in range(j + 1, BLOCK)}
            left[j] = left[j] * root
            right[j] = right[j] * root
            for i in range(j + 1, BLOCK):
                for k in range(j + 1, i + 1):
                    scalar[i, k] = scalar[i, k] - below[i] * below[k]
                left[i] = left[i] - below[i] * left[j]
                right[i] = right[i] - below[i] * right[j]
        for j in range(BLOCK):
            panel[j : j + 1, :n] = left[j][:1]
            panel[j : j + 1, n:] = right[j][:1]
        done = at + BLOCK
        upper_ref[at:done, :] = panel[:, :n]
        inverse_ref[at:done, :] = panel[:, n:]
        if done < n:
            one, two, three = split(panel[...])
            tall = jnp.concatenate([one, one, two, one, three, two], axis=0)
            other = jnp.concatenate([one, two, one, three, one, two], axis=0)
            change = multiply(tall[:, done:n], other, 0, 0)
            left_work[done:, :] = left_work[done:, :] - change[:, :n]
            right_work[done:, :] = right_work[done:, :] - change[:, n:]
    upper_ref[...] = jnp.where(columns >= rows, upper_ref[...], 0.0)


def factor_scratch(n):
    return [
        pltpu.VMEM((n, n), F32),
        pltpu.VMEM((n, n), F32),
        pltpu.VMEM((BLOCK, 2 * n), F32),
        pltpu.VMEM((BLOCK, BLOCK, n), F32),
    ]


def factor_kernel(gram_ref, upper_ref, inverse_ref, *work):
    factorize(gram_ref[...].reshape(upper_ref.shape), *work, upper_ref, inverse_ref)


def last_kernel(
    scale,
    basis, gram_ref, first_upper, modes_ref, factor_ref,
    upper, inverse, wide, narrow, staged, out_sem, *work,
):
    _, clon, clat, snaps = basis.shape
    factorize(gram_ref[...].reshape(upper.shape), *work, upper, inverse)
    set_weights(inverse[...].T * scale, wide, narrow)
    group = 8
    copies = []
    for which in range(3):
        for part in range(clon // group):
            start = part * group
            value = basis[which, start : start + group].reshape(group * clat, snaps)
            value = apply_weights(value, wide, narrow)
            for row in range(group):
                staged[:, which, start + row, :] = value[row * clat : (row + 1) * clat].T
            here = (slice(None), which, pl.ds(start, group), slice(None))
            copy = pltpu.make_async_copy(staged.at[here], modes_ref.at[here], out_sem.at[len(copies)])
            copy.start()
            copies.append(copy)
    factor_ref[...] = exact_dot(upper[...], first_upper[...], 1, 0) * (1.0 / scale)
    for copy in copies:
        copy.wait()


def whole(memory_space=pltpu.VMEM):
    return pl.BlockSpec(memory_space=memory_space)


def on_device(n_lon, n_lat, pressure, ocean_mask):
    snaps, clon, clat = pressure.shape
    n_a, _, _ = group_sizes(n_lon, n_lat)
    rows, wide = clon + 2 * MARGIN, clat + 2 * BASE
    mib = 1024 * 1024
    flat = jax.ShapeDtypeStruct((3, clon, clat, snaps), F32)
    pieces = jax.ShapeDtypeStruct((n_a, snaps // n_a, snaps), F32)
    square = jax.ShapeDtypeStruct((snaps, snaps), F32)
    weights = [pltpu.VMEM((2 * snaps, 2 * snaps), BF16), pltpu.VMEM((2 * snaps, snaps), BF16)]
    extended = pltpu.VMEM((rows, wide, snaps), F32)

    def params(limit, collective_id=None):
        more = {} if collective_id is None else {"collective_id": collective_id, "has_side_effects": True}
        return pltpu.CompilerParams(vmem_limit_bytes=limit * mib, **more)

    field, gram = pl.pallas_call(
        functools.partial(first_kernel, n_lon, n_lat),
        out_shape=(flat, pieces),
        in_specs=[whole(pltpu.HBM), whole(pltpu.HBM)],
        out_specs=(whole(), whole()),
        scratch_shapes=[pltpu.VMEM((snaps * clon, clat), F32)]
        + [pltpu.VMEM((clon, clat), jnp.int32), extended]
        + [pltpu.VMEM((clon + 2 * BASE, 3 * clat), F32)]
        + 5 * [extended]
        + reduce_scratch(n_lon, n_lat, snaps)
        + 2 * [pltpu.SemaphoreType.DMA((12,))]
        + 2 * [pltpu.SemaphoreType.DMA],
        compiler_params=params(32, 0),
        name="filter_gram",
    )(
        pltpu.with_memory_space_constraint(pressure.reshape(snaps * clon, clat), pltpu.HBM),
        pltpu.with_memory_space_constraint(ocean_mask, pltpu.HBM),
    )
    first_upper, first_inverse = pl.pallas_call(
        factor_kernel,
        out_shape=(square, square),
        in_specs=[whole()],
        out_specs=(whole(), whole()),
        scratch_shapes=factor_scratch(snaps),
        compiler_params=params(8),
        name="factor",
    )(gram)
    basis, gram = pl.pallas_call(
        functools.partial(second_kernel, n_lon, n_lat),
        out_shape=(flat, pieces),
        in_specs=[whole(), whole()],
        out_specs=(whole(), whole()),
        scratch_shapes=weights + reduce_scratch(n_lon, n_lat, snaps),
        compiler_params=params(20, 1),
        name="basis_gram",
    )(field, first_inverse)
    scale = float(3 * clon * clat * n_lon * n_lat) ** 0.5
    return pl.pallas_call(
        functools.partial(last_kernel, scale),
        out_shape=(jax.ShapeDtypeStruct((snaps, 3, clon, clat), F32), square),
        in_specs=[whole(), whole(), whole()],
        out_specs=(whole(pltpu.HBM), whole()),
        scratch_shapes=[pltpu.VMEM((snaps, snaps), F32)] * 2
        + weights
        + [pltpu.VMEM((snaps, 3, clon, clat), F32), pltpu.SemaphoreType.DMA((6,))]
        + factor_scratch(snaps),
        compiler_params=params(24),
        name="factor_modes",
    )(basis, gram, first_upper)


def solution(mesh):
    n_lon, n_lat = mesh.shape["lon"], mesh.shape["lat"]
    return jax.shard_map(
        functools.partial(on_device, n_lon, n_lat),
        mesh=mesh,
        in_specs=(P(None, "lon", "lat"), P("lon", "lat")),
        out_specs=(P(None, None, "lon", "lat"), P()),
        check_vma=False,
    )
```

```python
import functools

import jax
import jax.numpy as jnp
from jax import lax
from jax.experimental import pallas as pl
from jax.experimental.pallas import tpu as pltpu
from jax.sharding import PartitionSpec as P

PASSES = 4
MARGIN = PASSES + 1
CORES = 2
Y_LOW = 4
Y_HIGH = 2
BLOCK = 16
BASE = 8
MESH = pl.DeviceIdType.MESH
HIGHEST = lax.Precision.HIGHEST
F32, BF16 = jnp.float32, jnp.bfloat16


def steps_of(size):
    return sorted(range(1, size), key=lambda step: -min(step, size - step))


class Place:
    def __init__(self, n_lon, n_lat):
        self.n_lon, self.n_lat = n_lon, n_lat
        self.n_z = n_lon // (Y_LOW * CORES)
        self.n_y = Y_LOW * Y_HIGH
        self.n_x = n_lat // Y_HIGH
        self.n_a = self.n_x * CORES
        self.lon = lax.axis_index("lon")
        self.lat = lax.axis_index("lat")
        pair = lax.div(self.lon, CORES)
        self.core = lax.rem(self.lon, CORES)
        self.z = lax.div(pair, Y_LOW)
        self.x = lax.div(self.lat, Y_HIGH)
        self.y = lax.rem(self.lat, Y_HIGH) * Y_LOW + lax.rem(pair, Y_LOW)
        self.a = self.x * CORES + self.core

    def device(self, x, y, z, core):
        lon = (z * Y_LOW + lax.rem(y, Y_LOW)) * CORES + core
        return lon, x * Y_HIGH + lax.div(y, Y_LOW)

    def peer_a(self, step):
        rank = lax.rem(self.a + step, self.n_a)
        return rank, self.device(lax.div(rank, CORES), self.y, self.z, lax.rem(rank, CORES))

    def peer_y(self, step):
        rank = lax.rem(self.y + step, self.n_y)
        return rank, self.device(self.x, rank, self.z, self.core)

    def peer_z(self, step):
        rank = lax.rem(self.z + step, self.n_z)
        return rank, self.device(self.x, self.y, rank, self.core)

    def near(self, dlon, dlat):
        return (
            lax.rem(self.lon + dlon + self.n_lon, self.n_lon),
            lax.rem(self.lat + dlat + self.n_lat, self.n_lat),
        )

    def reduce_peers(self):
        groups = ((self.peer_a, self.n_a), (self.peer_y, self.n_y), (self.peer_z, self.n_z))
        return [peer(step)[1] for peer, size in groups for step in steps_of(size)]


def greet(devices):
    barrier = pltpu.get_barrier_semaphore()
    for device in devices:
        pl.semaphore_signal(barrier, inc=1, device_id=device, device_id_type=MESH)
    return len(devices)


def send(src, dst, send_sem, recv_sem, device):
    return pltpu.make_async_remote_copy(
        src_ref=src,
        dst_ref=dst,
        send_sem=send_sem,
        recv_sem=recv_sem,
        device_id=device,
        device_id_type=MESH,
    )


def exchange(peer, size, mine, source, target, sends, recvs):
    ranks = [peer(step) for step in steps_of(size)]
    started = [
        send(source(rank), target.at[mine], sends.at[rank], recvs.at[mine], device)
        for rank, device in ranks
    ]
    for copy in started:
        copy.start()

    def arrived():
        for rank, device in ranks:
            send(source(rank), target.at[rank], sends.at[rank], recvs.at[rank], device).wait_recv()

    def sent():
        for copy in started:
            copy.wait_send()

    return arrived, sent


def all_reduce(place, part, slots_a, slots_y, slots_z, total, sems):
    a, y, z = place.a, place.y, place.z
    arrived, sent_a = exchange(
        place.peer_a, place.n_a, a, lambda rank: part.at[rank], slots_a, sems[0], sems[1]
    )
    slots_a[a] = part[a]
    arrived()
    slots_y[y] = jnp.sum(slots_a[...], axis=0)
    arrived, sent_y = exchange(
        place.peer_y, place.n_y, y, lambda _: slots_y.at[y], slots_y, sems[2], sems[3]
    )
    arrived()
    slots_z[z] = jnp.sum(slots_y[...], axis=0)
    arrived, sent_z = exchange(
        place.peer_z, place.n_z, z, lambda _: slots_z.at[z], slots_z, sems[4], sems[5]
    )
    arrived()
    total[a] = jnp.sum(slots_z[...], axis=0)
    arrived, sent_b = exchange(
        place.peer_a, place.n_a, a, lambda _: total.at[a], total, sems[6], sems[7]
    )
    arrived()
    for sent in (sent_a, sent_y, sent_z, sent_b):
        sent()


def group_sizes(n_lon, n_lat):
    return n_lat // Y_HIGH * CORES, Y_LOW * Y_HIGH, n_lon // (Y_LOW * CORES)


def reduce_scratch(n_lon, n_lat, snaps):
    n_a, n_y, n_z = group_sizes(n_lon, n_lat)
    piece = (snaps // n_a, snaps)
    slots = [pltpu.VMEM((size, *piece), F32) for size in (n_a, n_a, n_y, n_z)]
    return slots + [pltpu.SemaphoreType.DMA((size,)) for size in (n_a, n_y, n_z, n_a) for _ in (0, 1)]


def split(value):
    one = value.astype(BF16)
    rest = value - one.astype(F32)
    two = rest.astype(BF16)
    return one, two, (rest - two.astype(F32)).astype(BF16)


def multiply(left, right, left_dim, right_dim):
    return lax.dot_general(
        left, right, (((left_dim,), (right_dim,)), ((), ())), preferred_element_type=F32
    )


def exact_dot(left, right, left_dim, right_dim):
    return lax.dot_general(
        left,
        right,
        (((left_dim,), (right_dim,)), ((), ())),
        precision=HIGHEST,
        preferred_element_type=F32,
    )


def set_weights(matrix, wide, narrow):
    one, two, three = split(matrix)
    pair = jnp.concatenate([one, two], axis=1)
    wide[...] = jnp.concatenate([pair, pair], axis=0)
    narrow[...] = jnp.concatenate([three, one], axis=0)


def apply_weights(value, wide, narrow):
    columns = value.shape[1]
    one, two, three = split(value)
    main = multiply(jnp.concatenate([one, two], axis=1), wide[...], 1, 0)
    rest = multiply(jnp.concatenate([one, three], axis=1), narrow[...], 1, 0)
    return main[:, :columns] + (main[:, columns:] + rest)


def apply_near_one(value, wide):
    columns = value.shape[1]
    one, two, _ = split(value)
    main = multiply(jnp.concatenate([one, two], axis=1), wide[...], 1, 0)
    return main[:, :columns] + main[:, columns:]


def gram_parts(value):
    one, two, three = split(value)
    pair = jnp.concatenate([one, two], axis=1)
    return multiply(pair, pair, 0, 0), multiply(one, three, 0, 0)


def gram_start(columns):
    return jnp.zeros((2 * columns, 2 * columns), F32), jnp.zeros((columns, columns), F32)


def gram_end(main, side):
    n = side.shape[0]
    cross = main[n:, :n] + main[:n, n:] + (main[n:, n:] + (side + side.T))
    return main[:n, :n] + cross


def span(delta, own_at, own, margin):
    if delta == 0:
        return pl.ds(own_at, own), pl.ds(own_at, own)
    if delta > 0:
        return pl.ds(own_at + own - margin, margin), pl.ds(own_at - margin, margin)
    return pl.ds(own_at, margin), pl.ds(own_at + own, margin)


def first_kernel(
    n_lon, n_lat,
    p_hbm, mask_hbm, flat, gram_ref,
    p_ref, mask_ref, raw, masks, even, odd, quarter, keep_lon, keep_lat,
    part, slots_a, slots_y, slots_z, *sems,
):
    reduce_sems, (near_send, near_recv, load_sem, mask_sem) = sems[:8], sems[8:]
    place = Place(n_lon, n_lat)
    clon, clat = mask_ref.shape
    snaps = raw.shape[2]
    wide = clat + 2 * BASE
    rows = clon + 2 * MARGIN
    load = pltpu.make_async_copy(p_hbm, p_ref, load_sem)
    load.start()
    load_mask = pltpu.make_async_copy(mask_hbm, mask_ref, mask_sem)
    load_mask.start()
    sides = [place.near(0, 1), place.near(0, -1), place.near(1, 0), place.near(-1, 0)]
    expected = greet(sides + place.reduce_peers())

    own_lon, own_lat = pl.ds(BASE, clon), pl.ds(clat, clat)
    load_mask.wait()
    masks[own_lon, own_lat] = mask_ref[...].astype(F32)
    load.wait()

    def turn(row):
        raw[MARGIN + row, BASE : BASE + clat, :] = p_ref[pl.ds(row, snaps, stride=clon), :].T

    for row in range(clon):
        turn(row)

    pl.semaphore_wait(pltpu.get_barrier_semaphore(), expected)

    def near(index, source, target, device):
        return send(source, target, near_send.at[index], near_recv.at[index], device)

    lat_mask, lat_field, lon_mask, lon_field, corners = [], [], [], [], []
    for index, delta in enumerate((1, -1)):
        device = place.near(0, delta)
        src, dst = span(delta, clat, clat, clat)
        lat_mask.append(
            near(index, masks.at[own_lon, own_lat], masks.at[own_lon, dst], device)
        )
        src, dst = span(delta, BASE, clat, MARGIN)
        inner = pl.ds(MARGIN, clon)
        lat_field.append(near(2 + index, raw.at[inner, src, :], raw.at[inner, dst, :], device))
    for index, delta in enumerate((1, -1)):
        device = place.near(delta, 0)
        src, dst = span(delta, BASE, clon, MARGIN)
        lon_mask.append(near(4 + index, masks.at[src, :], masks.at[dst, :], device))
        src, dst = span(delta, MARGIN, clon, MARGIN)
        inner = pl.ds(BASE, clat)
        lon_field.append(near(6 + index, raw.at[src, inner, :], raw.at[dst, inner, :], device))
        for end, at in enumerate((BASE - MARGIN, BASE + clat)):
            outer = pl.ds(at, MARGIN)
            number = 8 + 2 * index + end
            corners.append(near(number, raw.at[src, outer, :], raw.at[dst, outer, :], device))
    for copy in lat_mask + lat_field:
        copy.start()
    for copy in lat_field:
        copy.wait_send()
    for copy in lon_field:
        copy.start()
    for copy in lat_mask:
        copy.wait_recv()
    for copy in lon_mask:
        copy.start()
    for copy in lat_field:
        copy.wait_recv()
    for copy in corners:
        copy.start()
    for copy in lon_mask:
        copy.wait_recv()

    low = jnp.where(place.lat > 0, 1.0, 0.0)
    high = jnp.where(place.lat < n_lat - 1, 1.0, 0.0)
    turned = jnp.concatenate(
        [
            masks[:, 0:clat].T[clat - BASE :, :] * low,
            masks[:, clat : 2 * clat].T,
            masks[:, 2 * clat :].T[:BASE, :] * high,
        ],
        axis=0,
    )
    skip = BASE - MARGIN
    for row in range(rows):
        quarter[row] = 0.25 * jnp.broadcast_to(turned[:, row + skip : row + skip + 1], (wide, snaps))

    def coefficients(row, _):
        own = quarter[row]
        keep_lat[row] = 1.0 - (pltpu.roll(own, 1, 0) + pltpu.roll(own, wide - 1, 0))
        keep_lon[row] = 1.0 - (quarter[row - 1] + quarter[row + 1])
        return 0

    lax.fori_loop(1, rows - 1, coefficients, 0)

    def masked(row, _):
        even[row] = raw[row] * (4.0 * quarter[row])
        return 0

    def sweep(source, target, row):
        scale = quarter[row]
        lon_swept = source[row] * keep_lon[row] + scale * (source[row - 1] + source[row + 1])
        both = pltpu.roll(lon_swept, 1, 0) + pltpu.roll(lon_swept, wide - 1, 0)
        target[row] = lon_swept * keep_lat[row] + scale * both

    buffers = [(even, odd) if step % 2 == 0 else (odd, even) for step in range(PASSES)]
    first, last = MARGIN, MARGIN + clon
    lax.fori_loop(first, last, masked, 0)
    for step, (source, target) in enumerate(buffers):

        def inner_row(row, _, source=source, target=target):
            sweep(source, target, row)
            return 0

        lax.fori_loop(first + 1 + step, last - 1 - step, inner_row, 0)
    field = even if PASSES % 2 == 0 else odd

    def gradients(row, _):
        at = row + MARGIN
        half = 2.0 * quarter[at]
        centre = field[at]
        own = slice(BASE, BASE + clat)
        flat[0, row] = centre[own]
        flat[1, row] = (half * (field[at + 1] - field[at - 1]))[own]
        flat[2, row] = (half * (pltpu.roll(centre, wide - 1, 0) - pltpu.roll(centre, 1, 0)))[own]
        return 0

    def add_gram(carry, *ranges):
        for which in range(3):
            values = [flat[which, low:high].reshape(-1, snaps) for low, high in ranges]
            main, side = gram_parts(jnp.concatenate(values, axis=0))
            carry = carry[0] + main, carry[1] + side
        return carry

    low_end, high_start = MARGIN, clon - MARGIN
    lax.fori_loop(low_end, high_start, gradients, 0)
    carry = add_gram(gram_start(snaps), (low_end, high_start))
    for copy in lon_field + corners:
        copy.wait_recv()
    lax.fori_loop(0, first, masked, 0)
    lax.fori_loop(last, rows, masked, 0)
    for step, (source, target) in enumerate(buffers):

        def outer_rows(row, _, source=source, target=target, step=step):
            sweep(source, target, 1 + step + row)
            sweep(source, target, last - 1 - step + row)
            return 0

        lax.fori_loop(0, MARGIN, outer_rows, 0)
    lax.fori_loop(0, low_end, gradients, 0)
    lax.fori_loop(high_start, clon, gradients, 0)
    gram = gram_end(*add_gram(carry, (0, low_end), (high_start, clon)))
    part[...] = gram.reshape(part.shape)
    all_reduce(place, part, slots_a, slots_y, slots_z, gram_ref, reduce_sems)
    for copy in lat_mask + lon_mask + lon_field + corners:
        copy.wait_send()


def second_kernel(
    n_lon, n_lat,
    flat_ref, inverse_ref, basis, gram_ref,
    wide, narrow, part, slots_a, slots_y, slots_z, *sems,
):
    place = Place(n_lon, n_lat)
    expected = greet(place.reduce_peers())
    _, clon, clat, snaps = flat_ref.shape
    group = 16
    per = clon // group
    set_weights(inverse_ref[...].T, wide, narrow)

    def chunk(index, carry):
        which, where = lax.div(index, per), lax.rem(index, per) * group
        value = flat_ref[which, pl.ds(where, group)].reshape(group * clat, snaps)
        value = apply_weights(value, wide, narrow)
        basis[which, pl.ds(where, group)] = value.reshape(group, clat, snaps)
        main, side = gram_parts(value)
        return carry[0] + main, carry[1] + side

    gram = gram_end(*lax.fori_loop(0, 3 * per, chunk, gram_start(snaps), unroll=True))
    part[...] = gram.reshape(part.shape)
    pl.semaphore_wait(pltpu.get_barrier_semaphore(), expected)
    all_reduce(place, part, slots_a, slots_y, slots_z, gram_ref, sems)


def factorize(gram, left_work, right_work, panel, spread, upper_ref, inverse_ref):
    n = gram.shape[0]
    rows = lax.broadcasted_iota(jnp.int32, (n, n), 0)
    columns = lax.broadcasted_iota(jnp.int32, (n, n), 1)
    left_work[...] = gram
    right_work[...] = jnp.where(rows == columns, 1.0, 0.0)
    for at in range(0, n, BLOCK):
        for j in range(BLOCK):
            column = left_work[at : at + BLOCK, at + j : at + j + 1]
            spread[j] = jnp.broadcast_to(column, (BLOCK, n))

        def row_of(ref, i):
            return jnp.broadcast_to(ref[i : i + 1, :], (8, n))

        scalar = {
            (i, j): row_of(spread.at[j], i) for j in range(BLOCK) for i in range(j, BLOCK)
        }
        left = [row_of(left_work, at + i) for i in range(BLOCK)]
        right = [row_of(right_work, at + i) for i in range(BLOCK)]
        for j in range(BLOCK):
            root = lax.rsqrt(scalar[j, j])
            below = {i: scalar[i, j] * root for i in range(j + 1, BLOCK)}
            left[j] = left[j] * root
            right[j] = right[j] * root
            for i in range(j + 1, BLOCK):
                for k in range(j + 1, i + 1):
                    scalar[i, k] = scalar[i, k] - below[i] * below[k]
                left[i] = left[i] - below[i] * left[j]
                right[i] = right[i] - below[i] * right[j]
        for j in range(BLOCK):
            panel[j : j + 1, :n] = left[j][:1]
            panel[j : j + 1, n:] = right[j][:1]
        done = at + BLOCK
        upper_ref[at:done, :] = panel[:, :n]
        inverse_ref[at:done, :] = panel[:, n:]
        if done < n:
            one, two, three = split(panel[...])
            tall = jnp.concatenate([one, one, two, one, three, two], axis=0)
            other = jnp.concatenate([one, two, one, three, one, two], axis=0)
            change = multiply(tall[:, done:n], other, 0, 0)
            left_work[done:, :] = left_work[done:, :] - change[:, :n]
            right_work[done:, :] = right_work[done:, :] - change[:, n:]
    upper_ref[...] = jnp.where(columns >= rows, upper_ref[...], 0.0)


def factor_scratch(n):
    return [
        pltpu.VMEM((n, n), F32),
        pltpu.VMEM((n, n), F32),
        pltpu.VMEM((BLOCK, 2 * n), F32),
        pltpu.VMEM((BLOCK, BLOCK, n), F32),
    ]


def factor_kernel(gram_ref, upper_ref, inverse_ref, *work):
    factorize(gram_ref[...].reshape(upper_ref.shape), *work, upper_ref, inverse_ref)


def last_kernel(
    scale,
    basis, gram_ref, first_upper, modes_ref, factor_ref,
    upper, inverse, wide, narrow, staged, out_sem, *work,
):
    _, clon, clat, snaps = basis.shape
    factorize(gram_ref[...].reshape(upper.shape), *work, upper, inverse)
    set_weights(inverse[...].T * scale, wide, narrow)
    group = 4
    copies = []
    for which in range(3):
        for part in range(clon // group):
            start = part * group
            value = basis[which, start : start + group].reshape(group * clat, snaps)
            value = apply_near_one(value, wide)
            for row in range(group):
                staged[:, which, start + row, :] = value[row * clat : (row + 1) * clat].T
            here = (slice(None), which, pl.ds(start, group), slice(None))
            copy = pltpu.make_async_copy(staged.at[here], modes_ref.at[here], out_sem.at[len(copies)])
            copy.start()
            copies.append(copy)
    factor_ref[...] = exact_dot(upper[...], first_upper[...], 1, 0) * (1.0 / scale)
    for copy in copies:
        copy.wait()


def whole(memory_space=pltpu.VMEM):
    return pl.BlockSpec(memory_space=memory_space)


def on_device(n_lon, n_lat, pressure, ocean_mask):
    snaps, clon, clat = pressure.shape
    n_a, _, _ = group_sizes(n_lon, n_lat)
    rows, wide = clon + 2 * MARGIN, clat + 2 * BASE
    mib = 1024 * 1024
    flat = jax.ShapeDtypeStruct((3, clon, clat, snaps), F32)
    pieces = jax.ShapeDtypeStruct((n_a, snaps // n_a, snaps), F32)
    square = jax.ShapeDtypeStruct((snaps, snaps), F32)
    weights = [pltpu.VMEM((2 * snaps, 2 * snaps), BF16), pltpu.VMEM((2 * snaps, snaps), BF16)]
    extended = pltpu.VMEM((rows, wide, snaps), F32)

    def params(limit, collective_id=None):
        more = {} if collective_id is None else {"collective_id": collective_id, "has_side_effects": True}
        return pltpu.CompilerParams(vmem_limit_bytes=limit * mib, **more)

    field, gram = pl.pallas_call(
        functools.partial(first_kernel, n_lon, n_lat),
        out_shape=(flat, pieces),
        in_specs=[whole(pltpu.HBM), whole(pltpu.HBM)],
        out_specs=(whole(), whole()),
        scratch_shapes=[pltpu.VMEM((snaps * clon, clat), F32)]
        + [pltpu.VMEM((clon, clat), jnp.int32), extended]
        + [pltpu.VMEM((clon + 2 * BASE, 3 * clat), F32)]
        + 5 * [extended]
        + reduce_scratch(n_lon, n_lat, snaps)
        + 2 * [pltpu.SemaphoreType.DMA((12,))]
        + 2 * [pltpu.SemaphoreType.DMA],
        compiler_params=params(32, 0),
        name="filter_gram",
    )(
        pltpu.with_memory_space_constraint(pressure.reshape(snaps * clon, clat), pltpu.HBM),
        pltpu.with_memory_space_constraint(ocean_mask, pltpu.HBM),
    )
    first_upper, first_inverse = pl.pallas_call(
        factor_kernel,
        out_shape=(square, square),
        in_specs=[whole()],
        out_specs=(whole(), whole()),
        scratch_shapes=factor_scratch(snaps),
        compiler_params=params(8),
        name="factor",
    )(gram)
    basis, gram = pl.pallas_call(
        functools.partial(second_kernel, n_lon, n_lat),
        out_shape=(flat, pieces),
        in_specs=[whole(), whole()],
        out_specs=(whole(), whole()),
        scratch_shapes=weights + reduce_scratch(n_lon, n_lat, snaps),
        compiler_params=params(20, 1),
        name="basis_gram",
    )(field, first_inverse)
    scale = float(3 * clon * clat * n_lon * n_lat) ** 0.5
    return pl.pallas_call(
        functools.partial(last_kernel, scale),
        out_shape=(jax.ShapeDtypeStruct((snaps, 3, clon, clat), F32), square),
        in_specs=[whole(), whole(), whole()],
        out_specs=(whole(pltpu.HBM), whole()),
        scratch_shapes=[pltpu.VMEM((snaps, snaps), F32)] * 2
        + weights
        + [pltpu.VMEM((snaps, 3, clon, clat), F32), pltpu.SemaphoreType.DMA((3 * clon // 4,))]
        + factor_scratch(snaps),
        compiler_params=params(24),
        name="factor_modes",
    )(basis, gram, first_upper)


def solution(mesh):
    n_lon, n_lat = mesh.shape["lon"], mesh.shape["lat"]
    return jax.shard_map(
        functools.partial(on_device, n_lon, n_lat),
        mesh=mesh,
        in_specs=(P(None, "lon", "lat"), P("lon", "lat")),
        out_specs=(P(None, None, "lon", "lat"), P()),
        check_vma=False,
    )
```

```python
import functools

import jax
import jax.numpy as jnp
from jax import lax
from jax.experimental import pallas as pl
from jax.experimental.pallas import tpu as pltpu
from jax.sharding import PartitionSpec as P

PASSES = 4
MARGIN = PASSES + 1
CORES = 2
Y_LOW = 4
Y_HIGH = 2
BLOCK = 16
BASE = 8
MESH = pl.DeviceIdType.MESH
HIGHEST = lax.Precision.HIGHEST
F32, BF16 = jnp.float32, jnp.bfloat16


def steps_of(size):
    return sorted(range(1, size), key=lambda step: -min(step, size - step))


class Place:
    def __init__(self, n_lon, n_lat):
        self.n_lon, self.n_lat = n_lon, n_lat
        self.n_z = n_lon // (Y_LOW * CORES)
        self.n_y = Y_LOW * Y_HIGH
        self.n_x = n_lat // Y_HIGH
        self.n_a = self.n_x * CORES
        self.lon = lax.axis_index("lon")
        self.lat = lax.axis_index("lat")
        pair = lax.div(self.lon, CORES)
        self.core = lax.rem(self.lon, CORES)
        self.z = lax.div(pair, Y_LOW)
        self.x = lax.div(self.lat, Y_HIGH)
        self.y = lax.rem(self.lat, Y_HIGH) * Y_LOW + lax.rem(pair, Y_LOW)
        self.a = self.x * CORES + self.core

    def device(self, x, y, z, core):
        lon = (z * Y_LOW + lax.rem(y, Y_LOW)) * CORES + core
        return lon, x * Y_HIGH + lax.div(y, Y_LOW)

    def peer_a(self, step):
        rank = lax.rem(self.a + step, self.n_a)
        return rank, self.device(lax.div(rank, CORES), self.y, self.z, lax.rem(rank, CORES))

    def peer_y(self, step):
        rank = lax.rem(self.y + step, self.n_y)
        return rank, self.device(self.x, rank, self.z, self.core)

    def peer_z(self, step):
        rank = lax.rem(self.z + step, self.n_z)
        return rank, self.device(self.x, self.y, rank, self.core)

    def near(self, dlon, dlat):
        return (
            lax.rem(self.lon + dlon + self.n_lon, self.n_lon),
            lax.rem(self.lat + dlat + self.n_lat, self.n_lat),
        )

    def reduce_peers(self):
        groups = ((self.peer_a, self.n_a), (self.peer_y, self.n_y), (self.peer_z, self.n_z))
        return [peer(step)[1] for peer, size in groups for step in steps_of(size)]


def greet(devices):
    barrier = pltpu.get_barrier_semaphore()
    for device in devices:
        pl.semaphore_signal(barrier, inc=1, device_id=device, device_id_type=MESH)
    return len(devices)


def send(src, dst, send_sem, recv_sem, device):
    return pltpu.make_async_remote_copy(
        src_ref=src,
        dst_ref=dst,
        send_sem=send_sem,
        recv_sem=recv_sem,
        device_id=device,
        device_id_type=MESH,
    )


def exchange(peer, size, mine, source, target, sends, recvs):
    ranks = [peer(step) for step in steps_of(size)]
    started = [
        send(source(rank), target.at[mine], sends.at[rank], recvs.at[mine], device)
        for rank, device in ranks
    ]
    for copy in started:
        copy.start()

    def arrived():
        for rank, device in ranks:
            send(source(rank), target.at[rank], sends.at[rank], recvs.at[rank], device).wait_recv()

    def sent():
        for copy in started:
            copy.wait_send()

    return arrived, sent


def all_reduce(place, part, slots_a, slots_y, slots_z, total, sems):
    a, y, z = place.a, place.y, place.z
    arrived, sent_a = exchange(
        place.peer_a, place.n_a, a, lambda rank: part.at[rank], slots_a, sems[0], sems[1]
    )
    slots_a[a] = part[a]
    arrived()
    slots_y[y] = jnp.sum(slots_a[...], axis=0)
    arrived, sent_y = exchange(
        place.peer_y, place.n_y, y, lambda _: slots_y.at[y], slots_y, sems[2], sems[3]
    )
    arrived()
    slots_z[z] = jnp.sum(slots_y[...], axis=0)
    arrived, sent_z = exchange(
        place.peer_z, place.n_z, z, lambda _: slots_z.at[z], slots_z, sems[4], sems[5]
    )
    arrived()
    total[a] = jnp.sum(slots_z[...], axis=0)
    arrived, sent_b = exchange(
        place.peer_a, place.n_a, a, lambda _: total.at[a], total, sems[6], sems[7]
    )
    arrived()
    for sent in (sent_a, sent_y, sent_z, sent_b):
        sent()


def group_sizes(n_lon, n_lat):
    return n_lat // Y_HIGH * CORES, Y_LOW * Y_HIGH, n_lon // (Y_LOW * CORES)


def reduce_scratch(n_lon, n_lat, snaps):
    n_a, n_y, n_z = group_sizes(n_lon, n_lat)
    piece = (snaps // n_a, snaps)
    slots = [pltpu.VMEM((size, *piece), F32) for size in (n_a, n_a, n_y, n_z)]
    return slots + [pltpu.SemaphoreType.DMA((size,)) for size in (n_a, n_y, n_z, n_a) for _ in (0, 1)]


def split(value):
    one = value.astype(BF16)
    rest = value - one.astype(F32)
    two = rest.astype(BF16)
    return one, two, (rest - two.astype(F32)).astype(BF16)


def multiply(left, right, left_dim, right_dim):
    return lax.dot_general(
        left, right, (((left_dim,), (right_dim,)), ((), ())), preferred_element_type=F32
    )


def exact_dot(left, right, left_dim, right_dim):
    return lax.dot_general(
        left,
        right,
        (((left_dim,), (right_dim,)), ((), ())),
        precision=HIGHEST,
        preferred_element_type=F32,
    )


def set_weights(matrix, wide, narrow):
    one, two, three = split(matrix)
    pair = jnp.concatenate([one, two], axis=1)
    wide[...] = jnp.concatenate([pair, pair], axis=0)
    narrow[...] = jnp.concatenate([three, one], axis=0)


def apply_weights(value, wide, narrow):
    columns = value.shape[1]
    one, two, three = split(value)
    main = multiply(jnp.concatenate([one, two], axis=1), wide[...], 1, 0)
    rest = multiply(jnp.concatenate([one, three], axis=1), narrow[...], 1, 0)
    return main[:, :columns] + (main[:, columns:] + rest)


def apply_near_one(value, wide):
    columns = value.shape[1]
    one, two, _ = split(value)
    main = multiply(jnp.concatenate([one, two], axis=1), wide[...], 1, 0)
    return main[:, :columns] + main[:, columns:]


def gram_parts(value):
    one, two, three = split(value)
    pair = jnp.concatenate([one, two], axis=1)
    return multiply(pair, pair, 0, 0), multiply(one, three, 0, 0)


def gram_start(columns):
    return jnp.zeros((2 * columns, 2 * columns), F32), jnp.zeros((columns, columns), F32)


def gram_end(main, side):
    n = side.shape[0]
    cross = main[n:, :n] + main[:n, n:] + (main[n:, n:] + (side + side.T))
    return main[:n, :n] + cross


def span(delta, own_at, own, margin):
    if delta == 0:
        return pl.ds(own_at, own), pl.ds(own_at, own)
    if delta > 0:
        return pl.ds(own_at + own - margin, margin), pl.ds(own_at - margin, margin)
    return pl.ds(own_at, margin), pl.ds(own_at + own, margin)


def first_kernel(
    n_lon, n_lat,
    p_hbm, mask_hbm, flat, gram_ref,
    p_ref, mask_ref, raw, masks, even, odd, quarter, keep_lon, keep_lat,
    part, slots_a, slots_y, slots_z, *sems,
):
    reduce_sems, (near_send, near_recv, load_sem, mask_sem) = sems[:8], sems[8:]
    place = Place(n_lon, n_lat)
    clon, clat = mask_ref.shape
    snaps = raw.shape[2]
    wide = clat + 2 * BASE
    rows = clon + 2 * MARGIN
    load = pltpu.make_async_copy(p_hbm, p_ref, load_sem)
    load.start()
    load_mask = pltpu.make_async_copy(mask_hbm, mask_ref, mask_sem)
    load_mask.start()
    around = [(a, b) for a in (1, 0, -1) for b in (1, 0, -1) if (a, b) != (0, 0)]
    sides = [place.near(a, b) for a, b in around]
    expected = greet(sides + place.reduce_peers())

    own_lon, own_lat = pl.ds(BASE, clon), pl.ds(clat, clat)
    load_mask.wait()
    masks[own_lon, own_lat] = mask_ref[...].astype(F32)
    load.wait()

    def turn(row):
        raw[MARGIN + row, BASE : BASE + clat, :] = p_ref[pl.ds(row, snaps, stride=clon), :].T

    for row in range(clon):
        turn(row)

    pl.semaphore_wait(pltpu.get_barrier_semaphore(), expected)

    def near(index, source, target, device):
        return send(source, target, near_send.at[index], near_recv.at[index], device)

    mask_copies, lat_field, lon_field, corners = [], [], [], []
    for index, (a, b) in enumerate(around):
        src, dst = span(a, BASE, clon, MARGIN)
        _, columns = span(b, clat, clat, clat)
        source, target = masks.at[src, own_lat], masks.at[dst, columns]
        mask_copies.append(near(8 + index, source, target, place.near(a, b)))
    for index, delta in enumerate((1, -1)):
        src, dst = span(delta, BASE, clat, MARGIN)
        inner = pl.ds(MARGIN, clon)
        source, target = raw.at[inner, src, :], raw.at[inner, dst, :]
        lat_field.append(near(index, source, target, place.near(0, delta)))
    for index, delta in enumerate((1, -1)):
        device = place.near(delta, 0)
        src, dst = span(delta, MARGIN, clon, MARGIN)
        inner = pl.ds(BASE, clat)
        lon_field.append(near(2 + index, raw.at[src, inner, :], raw.at[dst, inner, :], device))
        for end, at in enumerate((BASE - MARGIN, BASE + clat)):
            outer = pl.ds(at, MARGIN)
            number = 4 + 2 * index + end
            corners.append(near(number, raw.at[src, outer, :], raw.at[dst, outer, :], device))
    for copy in mask_copies + lat_field:
        copy.start()
    for copy in lat_field:
        copy.wait_send()
    for copy in lon_field:
        copy.start()
    for copy in mask_copies:
        copy.wait_recv()

    low = jnp.where(place.lat > 0, 1.0, 0.0)
    high = jnp.where(place.lat < n_lat - 1, 1.0, 0.0)
    turned = jnp.concatenate(
        [
            masks[:, 0:clat].T[clat - BASE :, :] * low,
            masks[:, clat : 2 * clat].T,
            masks[:, 2 * clat :].T[:BASE, :] * high,
        ],
        axis=0,
    )
    skip = BASE - MARGIN
    for row in range(rows):
        quarter[row] = 0.25 * jnp.broadcast_to(turned[:, row + skip : row + skip + 1], (wide, snaps))

    def coefficients(row, _):
        own = quarter[row]
        keep_lat[row] = 1.0 - (pltpu.roll(own, 1, 0) + pltpu.roll(own, wide - 1, 0))
        keep_lon[row] = 1.0 - (quarter[row - 1] + quarter[row + 1])
        return 0

    lax.fori_loop(1, rows - 1, coefficients, 0)
    for copy in lat_field:
        copy.wait_recv()
    for copy in corners:
        copy.start()

    def masked(row, _):
        even[row] = raw[row] * (4.0 * quarter[row])
        return 0

    def sweep(source, target, row):
        scale = quarter[row]
        lon_swept = source[row] * keep_lon[row] + scale * (source[row - 1] + source[row + 1])
        both = pltpu.roll(lon_swept, 1, 0) + pltpu.roll(lon_swept, wide - 1, 0)
        target[row] = lon_swept * keep_lat[row] + scale * both

    buffers = [(even, odd) if step % 2 == 0 else (odd, even) for step in range(PASSES)]
    first, last = MARGIN, MARGIN + clon
    lax.fori_loop(first, last, masked, 0)
    for step, (source, target) in enumerate(buffers):

        def inner_row(row, _, source=source, target=target):
            sweep(source, target, row)
            return 0

        lax.fori_loop(first + 1 + step, last - 1 - step, inner_row, 0)
    field = even if PASSES % 2 == 0 else odd

    def gradients(row, _):
        at = row + MARGIN
        half = 2.0 * quarter[at]
        centre = field[at]
        own = slice(BASE, BASE + clat)
        flat[0, row] = centre[own]
        flat[1, row] = (half * (field[at + 1] - field[at - 1]))[own]
        flat[2, row] = (half * (pltpu.roll(centre, wide - 1, 0) - pltpu.roll(centre, 1, 0)))[own]
        return 0

    def add_gram(carry, *ranges):
        for which in range(3):
            values = [flat[which, low:high].reshape(-1, snaps) for low, high in ranges]
            main, side = gram_parts(jnp.concatenate(values, axis=0))
            carry = carry[0] + main, carry[1] + side
        return carry

    low_end, high_start = MARGIN, clon - MARGIN
    lax.fori_loop(low_end, high_start, gradients, 0)
    carry = add_gram(gram_start(snaps), (low_end, high_start))
    for copy in lon_field + corners:
        copy.wait_recv()
    lax.fori_loop(0, first, masked, 0)
    lax.fori_loop(last, rows, masked, 0)
    for step, (source, target) in enumerate(buffers):

        def outer_rows(row, _, source=source, target=target, step=step):
            sweep(source, target, 1 + step + row)
            sweep(source, target, last - 1 - step + row)
            return 0

        lax.fori_loop(0, MARGIN, outer_rows, 0)
    lax.fori_loop(0, low_end, gradients, 0)
    lax.fori_loop(high_start, clon, gradients, 0)
    gram = gram_end(*add_gram(carry, (0, low_end), (high_start, clon)))
    part[...] = gram.reshape(part.shape)
    all_reduce(place, part, slots_a, slots_y, slots_z, gram_ref, reduce_sems)
    for copy in mask_copies + lon_field + corners:
        copy.wait_send()


def second_kernel(
    n_lon, n_lat,
    flat_ref, inverse_ref, basis, gram_ref,
    wide, narrow, part, slots_a, slots_y, slots_z, *sems,
):
    place = Place(n_lon, n_lat)
    expected = greet(place.reduce_peers())
    _, clon, clat, snaps = flat_ref.shape
    group = 16
    per = clon // group
    set_weights(inverse_ref[...].T, wide, narrow)

    def chunk(index, carry):
        which, where = lax.div(index, per), lax.rem(index, per) * group
        value = flat_ref[which, pl.ds(where, group)].reshape(group * clat, snaps)
        value = apply_weights(value, wide, narrow)
        basis[which, pl.ds(where, group)] = value.reshape(group, clat, snaps)
        main, side = gram_parts(value)
        return carry[0] + main, carry[1] + side

    gram = gram_end(*lax.fori_loop(0, 3 * per, chunk, gram_start(snaps), unroll=True))
    part[...] = gram.reshape(part.shape)
    pl.semaphore_wait(pltpu.get_barrier_semaphore(), expected)
    all_reduce(place, part, slots_a, slots_y, slots_z, gram_ref, sems)


def factorize(gram, left_work, right_work, panel, spread, upper_ref, inverse_ref):
    n = gram.shape[0]
    rows = lax.broadcasted_iota(jnp.int32, (n, n), 0)
    columns = lax.broadcasted_iota(jnp.int32, (n, n), 1)
    left_work[...] = gram
    right_work[...] = jnp.where(rows == columns, 1.0, 0.0)
    for at in range(0, n, BLOCK):
        for j in range(BLOCK):
            column = left_work[at : at + BLOCK, at + j : at + j + 1]
            spread[j] = jnp.broadcast_to(column, (BLOCK, n))

        def row_of(ref, i):
            return jnp.broadcast_to(ref[i : i + 1, :], (8, n))

        scalar = {
            (i, j): row_of(spread.at[j], i) for j in range(BLOCK) for i in range(j, BLOCK)
        }
        left = [row_of(left_work, at + i) for i in range(BLOCK)]
        right = [row_of(right_work, at + i) for i in range(BLOCK)]
        for j in range(BLOCK):
            root = lax.rsqrt(scalar[j, j])
            below = {i: scalar[i, j] * root for i in range(j + 1, BLOCK)}
            left[j] = left[j] * root
            right[j] = right[j] * root
            for i in range(j + 1, BLOCK):
                for k in range(j + 1, i + 1):
                    scalar[i, k] = scalar[i, k] - below[i] * below[k]
                left[i] = left[i] - below[i] * left[j]
                right[i] = right[i] - below[i] * right[j]
        for j in range(BLOCK):
            panel[j : j + 1, :n] = left[j][:1]
            panel[j : j + 1, n:] = right[j][:1]
        done = at + BLOCK
        upper_ref[at:done, :] = panel[:, :n]
        inverse_ref[at:done, :] = panel[:, n:]
        if done < n:
            one, two, three = split(panel[...])
            tall = jnp.concatenate([one, one, two, one, three, two], axis=0)
            other = jnp.concatenate([one, two, one, three, one, two], axis=0)
            change = multiply(tall[:, done:n], other, 0, 0)
            left_work[done:, :] = left_work[done:, :] - change[:, :n]
            right_work[done:, :] = right_work[done:, :] - change[:, n:]
    upper_ref[...] = jnp.where(columns >= rows, upper_ref[...], 0.0)


def factor_scratch(n):
    return [
        pltpu.VMEM((n, n), F32),
        pltpu.VMEM((n, n), F32),
        pltpu.VMEM((BLOCK, 2 * n), F32),
        pltpu.VMEM((BLOCK, BLOCK, n), F32),
    ]


def factor_kernel(gram_ref, upper_ref, inverse_ref, *work):
    factorize(gram_ref[...].reshape(upper_ref.shape), *work, upper_ref, inverse_ref)


def last_kernel(
    scale,
    basis, gram_ref, first_upper, modes_ref, factor_ref,
    upper, inverse, wide, narrow, staged, out_sem, *work,
):
    _, clon, clat, snaps = basis.shape
    factorize(gram_ref[...].reshape(upper.shape), *work, upper, inverse)
    set_weights(inverse[...].T * scale, wide, narrow)
    group = 4
    copies = []
    for which in range(3):
        for part in range(clon // group):
            start = part * group
            value = basis[which, start : start + group].reshape(group * clat, snaps)
            value = apply_near_one(value, wide)
            for row in range(group):
                staged[:, which, start + row, :] = value[row * clat : (row + 1) * clat].T
            here = (slice(None), which, pl.ds(start, group), slice(None))
            copy = pltpu.make_async_copy(staged.at[here], modes_ref.at[here], out_sem.at[len(copies)])
            copy.start()
            copies.append(copy)
    factor_ref[...] = exact_dot(upper[...], first_upper[...], 1, 0) * (1.0 / scale)
    for copy in copies:
        copy.wait()


def whole(memory_space=pltpu.VMEM):
    return pl.BlockSpec(memory_space=memory_space)


def on_device(n_lon, n_lat, pressure, ocean_mask):
    snaps, clon, clat = pressure.shape
    n_a, _, _ = group_sizes(n_lon, n_lat)
    rows, wide = clon + 2 * MARGIN, clat + 2 * BASE
    mib = 1024 * 1024
    flat = jax.ShapeDtypeStruct((3, clon, clat, snaps), F32)
    pieces = jax.ShapeDtypeStruct((n_a, snaps // n_a, snaps), F32)
    square = jax.ShapeDtypeStruct((snaps, snaps), F32)
    weights = [pltpu.VMEM((2 * snaps, 2 * snaps), BF16), pltpu.VMEM((2 * snaps, snaps), BF16)]
    extended = pltpu.VMEM((rows, wide, snaps), F32)

    def params(limit, collective_id=None):
        more = {} if collective_id is None else {"collective_id": collective_id, "has_side_effects": True}
        return pltpu.CompilerParams(vmem_limit_bytes=limit * mib, **more)

    field, gram = pl.pallas_call(
        functools.partial(first_kernel, n_lon, n_lat),
        out_shape=(flat, pieces),
        in_specs=[whole(pltpu.HBM), whole(pltpu.HBM)],
        out_specs=(whole(), whole()),
        scratch_shapes=[pltpu.VMEM((snaps * clon, clat), F32)]
        + [pltpu.VMEM((clon, clat), jnp.int32), extended]
        + [pltpu.VMEM((clon + 2 * BASE, 3 * clat), F32)]
        + 5 * [extended]
        + reduce_scratch(n_lon, n_lat, snaps)
        + 2 * [pltpu.SemaphoreType.DMA((16,))]
        + 2 * [pltpu.SemaphoreType.DMA],
        compiler_params=params(32, 0),
        name="filter_gram",
    )(
        pltpu.with_memory_space_constraint(pressure.reshape(snaps * clon, clat), pltpu.HBM),
        pltpu.with_memory_space_constraint(ocean_mask, pltpu.HBM),
    )
    first_upper, first_inverse = pl.pallas_call(
        factor_kernel,
        out_shape=(square, square),
        in_specs=[whole()],
        out_specs=(whole(), whole()),
        scratch_shapes=factor_scratch(snaps),
        compiler_params=params(8),
        name="factor",
    )(gram)
    basis, gram = pl.pallas_call(
        functools.partial(second_kernel, n_lon, n_lat),
        out_shape=(flat, pieces),
        in_specs=[whole(), whole()],
        out_specs=(whole(), whole()),
        scratch_shapes=weights + reduce_scratch(n_lon, n_lat, snaps),
        compiler_params=params(20, 1),
        name="basis_gram",
    )(field, first_inverse)
    scale = float(3 * clon * clat * n_lon * n_lat) ** 0.5
    return pl.pallas_call(
        functools.partial(last_kernel, scale),
        out_shape=(jax.ShapeDtypeStruct((snaps, 3, clon, clat), F32), square),
        in_specs=[whole(), whole(), whole()],
        out_specs=(whole(pltpu.HBM), whole()),
        scratch_shapes=[pltpu.VMEM((snaps, snaps), F32)] * 2
        + weights
        + [pltpu.VMEM((snaps, 3, clon, clat), F32), pltpu.SemaphoreType.DMA((3 * clon // 4,))]
        + factor_scratch(snaps),
        compiler_params=params(24),
        name="factor_modes",
    )(basis, gram, first_upper)


def solution(mesh):
    n_lon, n_lat = mesh.shape["lon"], mesh.shape["lat"]
    return jax.shard_map(
        functools.partial(on_device, n_lon, n_lat),
        mesh=mesh,
        in_specs=(P(None, "lon", "lat"), P("lon", "lat")),
        out_specs=(P(None, None, "lon", "lat"), P()),
        check_vma=False,
    )
```

```python
import functools

import jax
import jax.numpy as jnp
from jax import lax
from jax.experimental import pallas as pl
from jax.experimental.pallas import tpu as pltpu
from jax.sharding import PartitionSpec as P

PASSES = 4
MARGIN = PASSES + 1
CORES = 2
Y_LOW = 4
Y_HIGH = 2
BLOCK = 16
BASE = 8
MESH = pl.DeviceIdType.MESH
HIGHEST = lax.Precision.HIGHEST
F32, BF16 = jnp.float32, jnp.bfloat16


def steps_of(size):
    return sorted(range(1, size), key=lambda step: -min(step, size - step))


class Place:
    def __init__(self, n_lon, n_lat):
        self.n_lon, self.n_lat = n_lon, n_lat
        self.n_z = n_lon // (Y_LOW * CORES)
        self.n_y = Y_LOW * Y_HIGH
        self.n_x = n_lat // Y_HIGH
        self.n_a = self.n_x * CORES
        self.lon = lax.axis_index("lon")
        self.lat = lax.axis_index("lat")
        pair = lax.div(self.lon, CORES)
        self.core = lax.rem(self.lon, CORES)
        self.z = lax.div(pair, Y_LOW)
        self.x = lax.div(self.lat, Y_HIGH)
        self.y = lax.rem(self.lat, Y_HIGH) * Y_LOW + lax.rem(pair, Y_LOW)
        self.a = self.x * CORES + self.core

    def device(self, x, y, z, core):
        lon = (z * Y_LOW + lax.rem(y, Y_LOW)) * CORES + core
        return lon, x * Y_HIGH + lax.div(y, Y_LOW)

    def peer_a(self, step):
        rank = lax.rem(self.a + step, self.n_a)
        return rank, self.device(lax.div(rank, CORES), self.y, self.z, lax.rem(rank, CORES))

    def peer_y(self, step):
        rank = lax.rem(self.y + step, self.n_y)
        return rank, self.device(self.x, rank, self.z, self.core)

    def peer_z(self, step):
        rank = lax.rem(self.z + step, self.n_z)
        return rank, self.device(self.x, self.y, rank, self.core)

    def near(self, dlon, dlat):
        return (
            lax.rem(self.lon + dlon + self.n_lon, self.n_lon),
            lax.rem(self.lat + dlat + self.n_lat, self.n_lat),
        )

    def reduce_peers(self):
        groups = ((self.peer_a, self.n_a), (self.peer_y, self.n_y), (self.peer_z, self.n_z))
        return [peer(step)[1] for peer, size in groups for step in steps_of(size)]


def greet(devices):
    barrier = pltpu.get_barrier_semaphore()
    for device in devices:
        pl.semaphore_signal(barrier, inc=1, device_id=device, device_id_type=MESH)
    return len(devices)


def send(src, dst, send_sem, recv_sem, device):
    return pltpu.make_async_remote_copy(
        src_ref=src,
        dst_ref=dst,
        send_sem=send_sem,
        recv_sem=recv_sem,
        device_id=device,
        device_id_type=MESH,
    )


def exchange(peer, size, mine, source, target, sends, recvs):
    ranks = [peer(step) for step in steps_of(size)]
    started = [
        send(source(rank), target.at[mine], sends.at[rank], recvs.at[mine], device)
        for rank, device in ranks
    ]
    for copy in started:
        copy.start()

    def arrived():
        for rank, device in ranks:
            send(source(rank), target.at[rank], sends.at[rank], recvs.at[rank], device).wait_recv()

    def sent():
        for copy in started:
            copy.wait_send()

    return arrived, sent


def all_reduce(place, part, slots_a, slots_y, slots_z, total, sems):
    a, y, z = place.a, place.y, place.z
    arrived, sent_a = exchange(
        place.peer_a, place.n_a, a, lambda rank: part.at[rank], slots_a, sems[0], sems[1]
    )
    slots_a[a] = part[a]
    arrived()
    slots_y[y] = jnp.sum(slots_a[...], axis=0)
    arrived, sent_y = exchange(
        place.peer_y, place.n_y, y, lambda _: slots_y.at[y], slots_y, sems[2], sems[3]
    )
    arrived()
    slots_z[z] = jnp.sum(slots_y[...], axis=0)
    arrived, sent_z = exchange(
        place.peer_z, place.n_z, z, lambda _: slots_z.at[z], slots_z, sems[4], sems[5]
    )
    arrived()
    total[a] = jnp.sum(slots_z[...], axis=0)
    arrived, sent_b = exchange(
        place.peer_a, place.n_a, a, lambda _: total.at[a], total, sems[6], sems[7]
    )
    arrived()
    for sent in (sent_a, sent_y, sent_z, sent_b):
        sent()


def group_sizes(n_lon, n_lat):
    return n_lat // Y_HIGH * CORES, Y_LOW * Y_HIGH, n_lon // (Y_LOW * CORES)


def reduce_scratch(n_lon, n_lat, snaps):
    n_a, n_y, n_z = group_sizes(n_lon, n_lat)
    piece = (snaps // n_a, snaps)
    slots = [pltpu.VMEM((size, *piece), F32) for size in (n_a, n_a, n_y, n_z)]
    return slots + [pltpu.SemaphoreType.DMA((size,)) for size in (n_a, n_y, n_z, n_a) for _ in (0, 1)]


def split(value):
    one = value.astype(BF16)
    rest = value - one.astype(F32)
    two = rest.astype(BF16)
    return one, two, (rest - two.astype(F32)).astype(BF16)


def multiply(left, right, left_dim, right_dim):
    return lax.dot_general(
        left, right, (((left_dim,), (right_dim,)), ((), ())), preferred_element_type=F32
    )


def exact_dot(left, right, left_dim, right_dim):
    return lax.dot_general(
        left,
        right,
        (((left_dim,), (right_dim,)), ((), ())),
        precision=HIGHEST,
        preferred_element_type=F32,
    )


def set_weights(matrix, wide, narrow):
    one, two, three = split(matrix)
    pair = jnp.concatenate([one, two], axis=1)
    wide[...] = jnp.concatenate([pair, pair], axis=0)
    narrow[...] = jnp.concatenate([three, one], axis=0)


def apply_weights(value, wide, narrow):
    columns = value.shape[1]
    one, two, three = split(value)
    main = multiply(jnp.concatenate([one, two], axis=1), wide[...], 1, 0)
    rest = multiply(jnp.concatenate([one, three], axis=1), narrow[...], 1, 0)
    return main[:, :columns] + (main[:, columns:] + rest)


def apply_near_one(value, wide):
    columns = value.shape[1]
    one, two, _ = split(value)
    main = multiply(jnp.concatenate([one, two], axis=1), wide[...], 1, 0)
    return main[:, :columns] + main[:, columns:]


def gram_parts(value):
    one, two, three = split(value)
    pair = jnp.concatenate([one, two], axis=1)
    return multiply(pair, pair, 0, 0), multiply(one, three, 0, 0)


def gram_start(columns):
    return jnp.zeros((2 * columns, 2 * columns), F32), jnp.zeros((columns, columns), F32)


def gram_end(main, side):
    n = side.shape[0]
    cross = main[n:, :n] + main[:n, n:] + (main[n:, n:] + (side + side.T))
    return main[:n, :n] + cross


def span(delta, own_at, own, margin):
    if delta == 0:
        return pl.ds(own_at, own), pl.ds(own_at, own)
    if delta > 0:
        return pl.ds(own_at + own - margin, margin), pl.ds(own_at - margin, margin)
    return pl.ds(own_at, margin), pl.ds(own_at + own, margin)


def first_kernel(
    n_lon, n_lat,
    p_hbm, mask_hbm, flat, gram_ref,
    p_ref, mask_ref, raw, masks, even, odd, quarter, keep_lon, keep_lat,
    part, slots_a, slots_y, slots_z, *sems,
):
    reduce_sems, (near_send, near_recv, load_sem, mask_sem) = sems[:8], sems[8:]
    place = Place(n_lon, n_lat)
    clon, clat = mask_ref.shape
    snaps = raw.shape[2]
    wide = clat + 2 * BASE
    rows = clon + 2 * MARGIN
    load = pltpu.make_async_copy(p_hbm, p_ref, load_sem)
    load.start()
    load_mask = pltpu.make_async_copy(mask_hbm, mask_ref, mask_sem)
    load_mask.start()
    around = [(a, b) for a in (1, 0, -1) for b in (1, 0, -1) if (a, b) != (0, 0)]
    sides = [place.near(a, b) for a, b in around]
    expected = greet(sides + place.reduce_peers())

    own_lon, own_lat = pl.ds(BASE, clon), pl.ds(clat, clat)
    load_mask.wait()
    masks[own_lon, own_lat] = mask_ref[...].astype(F32)
    load.wait()

    def turn(row):
        raw[MARGIN + row, BASE : BASE + clat, :] = p_ref[pl.ds(row, snaps, stride=clon), :].T

    for row in range(clon):
        turn(row)

    pl.semaphore_wait(pltpu.get_barrier_semaphore(), expected)

    def near(index, source, target, device):
        return send(source, target, near_send.at[index], near_recv.at[index], device)

    mask_copies, lat_field, lon_field, corners = [], [], [], []
    for index, (a, b) in enumerate(around):
        src, dst = span(a, BASE, clon, MARGIN)
        _, columns = span(b, clat, clat, clat)
        source, target = masks.at[src, own_lat], masks.at[dst, columns]
        mask_copies.append(near(8 + index, source, target, place.near(a, b)))
    for index, delta in enumerate((1, -1)):
        src, dst = span(delta, BASE, clat, MARGIN)
        inner = pl.ds(MARGIN, clon)
        source, target = raw.at[inner, src, :], raw.at[inner, dst, :]
        lat_field.append(near(index, source, target, place.near(0, delta)))
    for index, delta in enumerate((1, -1)):
        device = place.near(delta, 0)
        src, dst = span(delta, MARGIN, clon, MARGIN)
        inner = pl.ds(BASE, clat)
        lon_field.append(near(2 + index, raw.at[src, inner, :], raw.at[dst, inner, :], device))
        for end, at in enumerate((BASE - MARGIN, BASE + clat)):
            outer = pl.ds(at, MARGIN)
            number = 4 + 2 * index + end
            corners.append(near(number, raw.at[src, outer, :], raw.at[dst, outer, :], device))
    for copy in mask_copies + lat_field:
        copy.start()
    for copy in lat_field:
        copy.wait_send()
    for copy in lon_field:
        copy.start()
    for copy in mask_copies:
        copy.wait_recv()

    low = jnp.where(place.lat > 0, 1.0, 0.0)
    high = jnp.where(place.lat < n_lat - 1, 1.0, 0.0)
    turned = jnp.concatenate(
        [
            masks[:, 0:clat].T[clat - BASE :, :] * low,
            masks[:, clat : 2 * clat].T,
            masks[:, 2 * clat :].T[:BASE, :] * high,
        ],
        axis=0,
    )
    skip = BASE - MARGIN
    for row in range(rows):
        quarter[row] = 0.25 * jnp.broadcast_to(turned[:, row + skip : row + skip + 1], (wide, snaps))

    def coefficients(row, _):
        own = quarter[row]
        keep_lat[row] = 1.0 - (pltpu.roll(own, 1, 0) + pltpu.roll(own, wide - 1, 0))
        keep_lon[row] = 1.0 - (quarter[row - 1] + quarter[row + 1])
        return 0

    lax.fori_loop(1, rows - 1, coefficients, 0)
    for copy in lat_field:
        copy.wait_recv()
    for copy in corners:
        copy.start()

    def masked(row, _):
        even[row] = raw[row] * (4.0 * quarter[row])
        return 0

    def sweep(source, target, row):
        scale = quarter[row]
        lon_swept = source[row] * keep_lon[row] + scale * (source[row - 1] + source[row + 1])
        both = pltpu.roll(lon_swept, 1, 0) + pltpu.roll(lon_swept, wide - 1, 0)
        target[row] = lon_swept * keep_lat[row] + scale * both

    buffers = [(even, odd) if step % 2 == 0 else (odd, even) for step in range(PASSES)]
    first, last = MARGIN, MARGIN + clon
    lax.fori_loop(first, last, masked, 0)
    for step, (source, target) in enumerate(buffers):

        def inner_row(row, _, source=source, target=target):
            sweep(source, target, row)
            return 0

        lax.fori_loop(first + 1 + step, last - 1 - step, inner_row, 0)
    field = even if PASSES % 2 == 0 else odd

    def gradients(row, _):
        at = row + MARGIN
        half = 2.0 * quarter[at]
        centre = field[at]
        own = slice(BASE, BASE + clat)
        flat[0, row] = centre[own]
        flat[1, row] = (half * (field[at + 1] - field[at - 1]))[own]
        flat[2, row] = (half * (pltpu.roll(centre, wide - 1, 0) - pltpu.roll(centre, 1, 0)))[own]
        return 0

    def add_gram(carry, *ranges):
        for which in range(3):
            values = [flat[which, low:high].reshape(-1, snaps) for low, high in ranges]
            main, side = gram_parts(jnp.concatenate(values, axis=0))
            carry = carry[0] + main, carry[1] + side
        return carry

    low_end, high_start = MARGIN, clon - MARGIN
    lax.fori_loop(low_end, high_start, gradients, 0)
    carry = add_gram(gram_start(snaps), (low_end, high_start))
    for copy in lon_field + corners:
        copy.wait_recv()
    lax.fori_loop(0, first, masked, 0)
    lax.fori_loop(last, rows, masked, 0)
    for step, (source, target) in enumerate(buffers):

        def outer_rows(row, _, source=source, target=target, step=step):
            sweep(source, target, 1 + step + row)
            sweep(source, target, last - 1 - step + row)
            return 0

        lax.fori_loop(0, MARGIN, outer_rows, 0, unroll=True)
    lax.fori_loop(0, low_end, gradients, 0, unroll=True)
    lax.fori_loop(high_start, clon, gradients, 0, unroll=True)
    gram = gram_end(*add_gram(carry, (0, low_end), (high_start, clon)))
    part[...] = gram.reshape(part.shape)
    all_reduce(place, part, slots_a, slots_y, slots_z, gram_ref, reduce_sems)
    for copy in mask_copies + lon_field + corners:
        copy.wait_send()


def second_kernel(
    n_lon, n_lat,
    flat_ref, inverse_ref, basis, gram_ref,
    wide, narrow, part, slots_a, slots_y, slots_z, *sems,
):
    place = Place(n_lon, n_lat)
    expected = greet(place.reduce_peers())
    _, clon, clat, snaps = flat_ref.shape
    group = 16
    per = clon // group
    set_weights(inverse_ref[...].T, wide, narrow)

    def chunk(index, carry):
        which, where = lax.div(index, per), lax.rem(index, per) * group
        value = flat_ref[which, pl.ds(where, group)].reshape(group * clat, snaps)
        value = apply_weights(value, wide, narrow)
        basis[which, pl.ds(where, group)] = value.reshape(group, clat, snaps)
        main, side = gram_parts(value)
        return carry[0] + main, carry[1] + side

    gram = gram_end(*lax.fori_loop(0, 3 * per, chunk, gram_start(snaps), unroll=True))
    part[...] = gram.reshape(part.shape)
    pl.semaphore_wait(pltpu.get_barrier_semaphore(), expected)
    all_reduce(place, part, slots_a, slots_y, slots_z, gram_ref, sems)


def factorize(gram, left_work, right_work, panel, spread, upper_ref, inverse_ref):
    n = gram.shape[0]
    rows = lax.broadcasted_iota(jnp.int32, (n, n), 0)
    columns = lax.broadcasted_iota(jnp.int32, (n, n), 1)
    left_work[...] = gram
    right_work[...] = jnp.where(rows == columns, 1.0, 0.0)
    for at in range(0, n, BLOCK):
        for j in range(BLOCK):
            column = left_work[at : at + BLOCK, at + j : at + j + 1]
            spread[j] = jnp.broadcast_to(column, (BLOCK, n))

        def row_of(ref, i):
            return jnp.broadcast_to(ref[i : i + 1, :], (8, n))

        scalar = {
            (i, j): row_of(spread.at[j], i) for j in range(BLOCK) for i in range(j, BLOCK)
        }
        left = [row_of(left_work, at + i) for i in range(BLOCK)]
        right = [row_of(right_work, at + i) for i in range(BLOCK)]
        for j in range(BLOCK):
            root = lax.rsqrt(scalar[j, j])
            below = {i: scalar[i, j] * root for i in range(j + 1, BLOCK)}
            left[j] = left[j] * root
            right[j] = right[j] * root
            for i in range(j + 1, BLOCK):
                for k in range(j + 1, i + 1):
                    scalar[i, k] = scalar[i, k] - below[i] * below[k]
                left[i] = left[i] - below[i] * left[j]
                right[i] = right[i] - below[i] * right[j]
        for j in range(BLOCK):
            panel[j : j + 1, :n] = left[j][:1]
            panel[j : j + 1, n:] = right[j][:1]
        done = at + BLOCK
        upper_ref[at:done, :] = panel[:, :n]
        inverse_ref[at:done, :] = panel[:, n:]
        if done < n:
            one, two, three = split(panel[...])
            tall = jnp.concatenate([one, one, two, one, three, two], axis=0)
            other = jnp.concatenate([one, two, one, three, one, two], axis=0)
            change = multiply(tall[:, done:n], other, 0, 0)
            left_work[done:, :] = left_work[done:, :] - change[:, :n]
            right_work[done:, :] = right_work[done:, :] - change[:, n:]
    upper_ref[...] = jnp.where(columns >= rows, upper_ref[...], 0.0)


def factor_scratch(n):
    return [
        pltpu.VMEM((n, n), F32),
        pltpu.VMEM((n, n), F32),
        pltpu.VMEM((BLOCK, 2 * n), F32),
        pltpu.VMEM((BLOCK, BLOCK, n), F32),
    ]


def factor_kernel(gram_ref, upper_ref, inverse_ref, *work):
    factorize(gram_ref[...].reshape(upper_ref.shape), *work, upper_ref, inverse_ref)


def last_kernel(
    scale,
    basis, gram_ref, first_upper, modes_ref, factor_ref,
    upper, inverse, wide, narrow, staged, out_sem, *work,
):
    _, clon, clat, snaps = basis.shape
    factorize(gram_ref[...].reshape(upper.shape), *work, upper, inverse)
    set_weights(inverse[...].T * scale, wide, narrow)
    group = 4
    copies = []
    for which in range(3):
        for part in range(clon // group):
            start = part * group
            value = basis[which, start : start + group].reshape(group * clat, snaps)
            value = apply_near_one(value, wide)
            for row in range(group):
                staged[:, which, start + row, :] = value[row * clat : (row + 1) * clat].T
            here = (slice(None), which, pl.ds(start, group), slice(None))
            copy = pltpu.make_async_copy(staged.at[here], modes_ref.at[here], out_sem.at[len(copies)])
            copy.start()
            copies.append(copy)
    factor_ref[...] = exact_dot(upper[...], first_upper[...], 1, 0) * (1.0 / scale)
    for copy in copies:
        copy.wait()


def whole(memory_space=pltpu.VMEM):
    return pl.BlockSpec(memory_space=memory_space)


def on_device(n_lon, n_lat, pressure, ocean_mask):
    snaps, clon, clat = pressure.shape
    n_a, _, _ = group_sizes(n_lon, n_lat)
    rows, wide = clon + 2 * MARGIN, clat + 2 * BASE
    mib = 1024 * 1024
    flat = jax.ShapeDtypeStruct((3, clon, clat, snaps), F32)
    pieces = jax.ShapeDtypeStruct((n_a, snaps // n_a, snaps), F32)
    square = jax.ShapeDtypeStruct((snaps, snaps), F32)
    weights = [pltpu.VMEM((2 * snaps, 2 * snaps), BF16), pltpu.VMEM((2 * snaps, snaps), BF16)]
    extended = pltpu.VMEM((rows, wide, snaps), F32)

    def params(limit, collective_id=None):
        more = {} if collective_id is None else {"collective_id": collective_id, "has_side_effects": True}
        return pltpu.CompilerParams(vmem_limit_bytes=limit * mib, **more)

    field, gram = pl.pallas_call(
        functools.partial(first_kernel, n_lon, n_lat),
        out_shape=(flat, pieces),
        in_specs=[whole(pltpu.HBM), whole(pltpu.HBM)],
        out_specs=(whole(), whole()),
        scratch_shapes=[pltpu.VMEM((snaps * clon, clat), F32)]
        + [pltpu.VMEM((clon, clat), jnp.int32), extended]
        + [pltpu.VMEM((clon + 2 * BASE, 3 * clat), F32)]
        + 5 * [extended]
        + reduce_scratch(n_lon, n_lat, snaps)
        + 2 * [pltpu.SemaphoreType.DMA((16,))]
        + 2 * [pltpu.SemaphoreType.DMA],
        compiler_params=params(32, 0),
        name="filter_gram",
    )(
        pltpu.with_memory_space_constraint(pressure.reshape(snaps * clon, clat), pltpu.HBM),
        pltpu.with_memory_space_constraint(ocean_mask, pltpu.HBM),
    )
    first_upper, first_inverse = pl.pallas_call(
        factor_kernel,
        out_shape=(square, square),
        in_specs=[whole()],
        out_specs=(whole(), whole()),
        scratch_shapes=factor_scratch(snaps),
        compiler_params=params(8),
        name="factor",
    )(gram)
    basis, gram = pl.pallas_call(
        functools.partial(second_kernel, n_lon, n_lat),
        out_shape=(flat, pieces),
        in_specs=[whole(), whole()],
        out_specs=(whole(), whole()),
        scratch_shapes=weights + reduce_scratch(n_lon, n_lat, snaps),
        compiler_params=params(20, 1),
        name="basis_gram",
    )(field, first_inverse)
    scale = float(3 * clon * clat * n_lon * n_lat) ** 0.5
    return pl.pallas_call(
        functools.partial(last_kernel, scale),
        out_shape=(jax.ShapeDtypeStruct((snaps, 3, clon, clat), F32), square),
        in_specs=[whole(), whole(), whole()],
        out_specs=(whole(pltpu.HBM), whole()),
        scratch_shapes=[pltpu.VMEM((snaps, snaps), F32)] * 2
        + weights
        + [pltpu.VMEM((snaps, 3, clon, clat), F32), pltpu.SemaphoreType.DMA((3 * clon // 4,))]
        + factor_scratch(snaps),
        compiler_params=params(24),
        name="factor_modes",
    )(basis, gram, first_upper)


def solution(mesh):
    n_lon, n_lat = mesh.shape["lon"], mesh.shape["lat"]
    return jax.shard_map(
        functools.partial(on_device, n_lon, n_lat),
        mesh=mesh,
        in_specs=(P(None, "lon", "lat"), P("lon", "lat")),
        out_specs=(P(None, None, "lon", "lat"), P()),
        check_vma=False,
    )
```
